32 devices in a mesh: dp: 8 (over z, core), expert: 4 (over y, x).
Axes of the slice: x: 2, y: 2, z: 4, core: 2. Of those that a mesh axis runs over, the one named last changes fastest.
Arguments:
- tokens: bfloat16 [32768, 768], P(('dp', 'expert')), may hold values from -6 to 6
- segment_ids: int32 [32, 1024], P(('dp', 'expert')), may hold values from 0 to 3, never falling along the last dimension, each value on 1 to 512 neighbouring positions
- expert_order: int32 [32768], P(('dp', 'expert')), may hold values from 0 to 1023, as said below
- expert_counts: int32 [32, 8], P(('dp', 'expert')), may hold values from 0 to 256, as said below
- norm1_gain: float32 [768], replicated, may hold values from 0.5 to 1.5
- norm1_bias: float32 [768], replicated, may hold values from -0.5 to 0.5
- query_w: bfloat16 [768, 768], replicated, may hold values from -0.3125 to 0.3125
- key_w: bfloat16 [768, 768], replicated, may hold values from -0.3125 to 0.3125
- value_w: bfloat16 [768, 768], replicated, may hold values from -0.21875 to 0.21875
- out_w: bfloat16 [768, 768], replicated, may hold values from -0.625 to 0.625
- norm2_gain: float32 [768], replicated, may hold values from 0.5 to 1.5
- norm2_bias: float32 [768], replicated, may hold values from -0.5 to 0.5
- router_w: bfloat16 [768, 8], replicated, may hold values from -0.15625 to 0.15625
- expert_in: bfloat16 [8, 768, 3072], P('expert'), may hold values from -0.21875 to 0.21875
- expert_out: bfloat16 [8, 3072, 768], P('expert'), may hold values from -0.3125 to 0.3125
- cotangent: bfloat16 [32768, 768], P(('dp', 'expert')), may hold values from -8 to 8
Outputs:
- block_out: bfloat16 [32768, 768], P(('dp', 'expert'))
- tokens_grad: bfloat16 [32768, 768], P(('dp', 'expert'))
- norm1_gain_grad: float32 [768], replicated
- norm1_bias_grad: float32 [768], replicated
- query_grad: float32 [768, 768], replicated
- key_grad: float32 [768, 768], replicated
- value_grad: float32 [768, 768], replicated
- out_grad: float32 [768, 768], replicated
- norm2_gain_grad: float32 [768], replicated
- norm2_bias_grad: float32 [768], replicated
- expert_in_grad: float32 [8, 768, 3072], P('expert', 'dp')
- expert_out_grad: float32 [8, 3072, 768], P('expert', 'dp')
The draws below stay inside these ranges and needn't reach their ends.
Inputs may be any that keep to these rules, and one draw needn't show every extreme that they name: `segment_ids`: each row holds 4 documents in order, each of 1 to 512 positions. `expert_order`: each block of 1024 entries (one device's tokens) holds every number 0 to 1023 once; its p-th entry is the token that stands p-th when that device's tokens are ordered by expert. `expert_counts`: row d counts device d's tokens for each expert and sums to 1024; no count exceeds 256, and one expert, the same in every row, has exactly 256 in every row.
All inputs are finite; a program needn't handle non-finite values.
Results may differ from the reference program's by a relative error of at most 0.015.
Values may be sent and summed in bfloat16 or wider, within the bound.
No kernel may reach another device: no remote copies, remote signals or barrier semaphores. Data moves between devices by JAX's collectives and lax.ppermute only.
A program may use at most 320 MiB of HBM per device.

```python
import math
import jax
import jax.numpy as jnp
import numpy as np
from jax import lax

D = 768
FF = 3072
HEADS = 12
HEAD_DIM = 64
LEN = 1024
SEGS = 4
TOK_DEV = 1024
SEQS = 32
TOKENS = 32768
EXPERTS = 8
CAP = 256
SEG_MOST = 512
DEVICES = 32


def route_table(key):
    key_hot, key_slope, key_noise, key_order = jax.random.split(key, 4)
    others = EXPERTS - 1
    hot_expert = jax.random.randint(key_hot, (), 0, EXPERTS)
    slopes = jax.random.randint(key_slope, (DEVICES, others, 1), 1, 9)
    noise = jax.random.randint(key_noise, (DEVICES, others, CAP), 0, CAP)
    slot_rank = lax.broadcasted_iota(jnp.int32, (DEVICES, others, CAP), 2)
    places = lax.broadcasted_iota(jnp.int32, (DEVICES, others * CAP), 1)
    scores = (noise - slot_rank * slopes + 9 * CAP).reshape(DEVICES, others * CAP)
    keyed = scores * (others * CAP) + places
    _, picked = lax.top_k(keyed, TOK_DEV - CAP)
    owner = picked // CAP
    tally = jnp.sum((owner[:, :, None] == lax.broadcasted_iota(jnp.int32, (1, 1, others), 2)).astype(jnp.int32), axis=1)
    columns = lax.iota(jnp.int32, EXPERTS)
    source = jnp.clip(columns - (columns > hot_expert).astype(jnp.int32), 0, others - 1)
    counts = jnp.where(columns[None, :] == hot_expert, CAP, tally[:, source])
    limit = 2 ** 30 // TOK_DEV
    draws = jax.random.randint(key_order, (DEVICES, TOK_DEV), 0, limit)
    order = jnp.argsort(draws * TOK_DEV + lax.broadcasted_iota(jnp.int32, (DEVICES, TOK_DEV), 1), axis=1)
    return (order.astype(jnp.int32), counts.astype(jnp.int32))


def draw_expert_order(key, part):
    order, _ = route_table(jax.random.fold_in(key, 17))
    return order.reshape(TOKENS)


def draw_expert_counts(key, part):
    _, counts = route_table(jax.random.fold_in(key, 17))
    return counts


def draw_cotangent(key, part):
    device_of = (lax.broadcasted_iota(jnp.int32, (TOKENS, 1), 0) // TOK_DEV).astype(jnp.float32)
    row_scale = 0.6 * jnp.exp(jnp.log(3.0) * device_of / (DEVICES - 1))
    values = jax.random.truncated_normal(key, -4.0, 4.0, (TOKENS, D), jnp.float32)
    return (values * row_scale).astype(jnp.bfloat16)


def levels(key, dims, pieces, smallest, largest):
    def one(dim, parts):
        heights = jax.random.uniform(jax.random.fold_in(jax.random.fold_in(key, 6), dim), (parts,), jnp.float32, smallest / len(pieces), largest / len(pieces))
        return jnp.repeat(jnp.exp(heights), dims[dim] // parts).reshape((-1,) + (1,) * (len(dims) - dim - 1))

    loudness = one(*pieces[0])
    for cut in pieces[1:]:
        loudness = loudness * one(*cut)
    return loudness


def length_profile(number_of, total, bound, slope):
    portions = [(1 << 20) // math.isqrt(rank ** slope) + 1 for rank in range(2, number_of + 1)]
    spare, holding = total - bound - (number_of - 1), [1] * (number_of - 1)
    while spare > 0:
        free = [i for i in range(number_of - 1) if holding[i] < bound]
        whole, remaining = sum([portions[i] for i in free]), spare
        for i in free:
            extra = min(bound - holding[i], max(1, remaining * portions[i] // whole), spare)
            holding[i] = holding[i] + extra
            spare = spare - extra
    return np.array([bound] + holding)


def ragged_sizes(stream_key, count, total, bound, skew):
    if count == 2:
        one = jax.random.randint(stream_key, (), max(1, total - bound), min(bound, total - 1) + 1)
        return jnp.stack([one, total - one])
    lengths = jnp.asarray(length_profile(count, total, bound, skew), jnp.int32)
    pairs = (count - 1) // 2
    giver, sink = lengths[1:1 + 2 * pairs:2], lengths[2:2 + 2 * pairs:2]
    margin = jnp.minimum(giver - 1, bound - sink)
    shifted = jax.random.randint(jax.random.fold_in(stream_key, 1), (pairs,), 0, 1 << 20) % (margin + 1)
    lengths = lengths.at[1:1 + 2 * pairs:2].set(giver - shifted).at[2:2 + 2 * pairs:2].set(sink + shifted)
    return lengths[jax.random.permutation(jax.random.fold_in(stream_key, 2), count)]


def centred(stream_key, shape, spread, most, cuts=(), dtype=jnp.bfloat16):
    drawn = jax.random.normal(stream_key, shape, jnp.float32) * spread
    if len(cuts) > 0:
        drawn = levels(stream_key, shape, cuts, -0.22, 0.18) * drawn
    return jnp.clip(drawn, min=-most, max=most).astype(dtype)


def setup_inputs(seed: int = 0) -> dict:
    arg_keys = jax.random.split(jax.random.key(seed), 17)
    return {
        "tokens": centred(arg_keys[0], (TOKENS, D), 1.0, 6.0, ((0, 32),)),
        "segment_ids": jax.vmap(lambda own: jnp.searchsorted(jnp.cumsum(ragged_sizes(own, SEGS, LEN, SEG_MOST, 2)), jnp.arange(LEN), side="right"))(jax.random.split(arg_keys[1], SEQS)).reshape((SEQS, LEN)).astype(jnp.int32),
        "expert_order": draw_expert_order(jax.random.fold_in(arg_keys[16], 71), 0),
        "expert_counts": draw_expert_counts(jax.random.fold_in(arg_keys[16], 71), 0),
        "norm1_gain": jnp.clip(1.0 + 0.1 * jax.random.normal(arg_keys[4], (D,), jnp.float32), 0.5, 1.5),
        "norm1_bias": centred(arg_keys[5], (D,), 0.1, 0.5, (), jnp.float32),
        "query_w": centred(arg_keys[6], (D, D), (D // 2) ** -0.5, 0.3125),
        "key_w": centred(arg_keys[7], (D, D), (D // 2) ** -0.5, 0.3125),
        "value_w": centred(arg_keys[8], (D, D), D ** -0.5, 0.21875),
        "out_w": centred(arg_keys[9], (D, D), (D // 8) ** -0.5, 0.625),
        "norm2_gain": jnp.clip(1.0 + 0.1 * jax.random.normal(arg_keys[10], (D,), jnp.float32), 0.5, 1.5),
        "norm2_bias": centred(arg_keys[11], (D,), 0.1, 0.5, (), jnp.float32),
        "router_w": centred(arg_keys[12], (D, EXPERTS), (2 * D) ** -0.5, 0.15625),
        "expert_in": centred(arg_keys[13], (EXPERTS, D, FF), D ** -0.5, 0.21875, ((0, 4),)),
        "expert_out": centred(arg_keys[14], (EXPERTS, FF, D), (FF // 8) ** -0.5, 0.3125, ((0, 4),)),
        "cotangent": draw_cotangent(jax.random.fold_in(arg_keys[16], 71), 0),
    }


EPSILON = 1e-05
NEG_LARGE = -1e+30
PRECISE = lax.Precision.HIGHEST

@jax.custom_vjp
def low(v):
    return lax.optimization_barrier(v.astype(jnp.bfloat16)).astype(jnp.float32)

@jax.custom_vjp
def low_back(v):
    return v

def low_keep(v):
    return (low(v), None)

def low_pass(kept, grad):
    return (grad,)

def back_keep(v):
    return (v, None)

def back_low(kept, grad):
    return (low(grad),)
low.defvjp(low_keep, low_pass)
low_back.defvjp(back_keep, back_low)

def layer_norm(values, gain_vec, bias_vec):
    centered = values - lax.optimization_barrier(jnp.mean(values, axis=-1, keepdims=True))
    inverse_std = lax.rsqrt(lax.optimization_barrier(jnp.mean(centered * centered, axis=-1, keepdims=True)) + EPSILON)
    return centered * inverse_std * gain_vec + bias_vec

def matmul(left, right):
    return jnp.dot(left, right, precision=PRECISE, preferred_element_type=jnp.float32)

def attend_sequence(packed):
    queries, key_rows, value_rows, segments = packed
    length = queries.shape[0]
    query_heads = queries.reshape(length, HEADS, HEAD_DIM)
    key_heads = key_rows.reshape(length, HEADS, HEAD_DIM)
    value_heads = value_rows.reshape(length, HEADS, HEAD_DIM)
    scores = low_back(jnp.einsum('qhd,khd->hqk', query_heads, key_heads, precision=PRECISE) * HEAD_DIM ** (-0.5))
    places = lax.iota(jnp.int32, length)
    allowed = (segments[None, :] == segments[:, None]) & (places[None, :] <= places[:, None])
    scores = jnp.where(allowed[None], scores, NEG_LARGE)
    row_max = lax.optimization_barrier(jnp.max(scores, axis=-1, keepdims=True))
    weights = jnp.exp(scores - row_max)
    attn_prob = low(weights / lax.optimization_barrier(jnp.sum(weights, axis=-1, keepdims=True)))
    mixture = jnp.einsum('hqk,khd->qhd', attn_prob, value_heads, precision=PRECISE)
    return low_back(low(mixture.reshape(length, HEADS * HEAD_DIM)))

def expert_apply(packed):
    row_block, first_w, second_w = packed
    pre_act = low_back(matmul(row_block, first_w))
    hidden_act = low(jax.nn.gelu(pre_act, approximate=False))
    return low_back(low(matmul(hidden_act, second_w)))

def route_indices(expert_order, expert_counts):
    devices, experts = expert_counts.shape
    tok_count = expert_order.shape[0] // devices
    order = expert_order.reshape(devices, tok_count)
    upper_end = jnp.cumsum(expert_counts, axis=1)
    lower_end = upper_end - expert_counts
    slot_rank = lax.iota(jnp.int32, CAP)
    positions = jnp.minimum(lower_end[:, :, None] + slot_rank[None, None, :], tok_count - 1).reshape(devices, experts * CAP)
    local_rows = jnp.take_along_axis(order, positions, axis=1)
    device_ids = lax.iota(jnp.int32, devices)
    row_ids = (local_rows + (device_ids * tok_count)[:, None]).reshape(devices, experts, CAP)
    filled = slot_rank[None, None, :] < expert_counts[:, :, None]
    ranks = jnp.broadcast_to(lax.iota(jnp.int32, tok_count)[None, :], (devices, tok_count))
    inverse = jnp.zeros((devices, tok_count), jnp.int32).at[device_ids[:, None], order].set(ranks)
    expert_of = lax.optimization_barrier(jnp.sum((upper_end[:, None, :] <= inverse[:, :, None]).astype(jnp.int32), axis=2))
    first_slot = jnp.take_along_axis(lower_end, expert_of, axis=1)
    flat_rows = expert_of * (devices * CAP) + device_ids[:, None] * CAP + inverse - first_slot
    return (row_ids, filled, expert_of.reshape(-1), flat_rows.reshape(-1))

def reference(tokens, segment_ids, expert_order, expert_counts, norm1_gain, norm1_bias, query_w, key_w, value_w, out_w, norm2_gain, norm2_bias, router_w, expert_in, expert_out, cotangent):
    row_ids, filled, expert_of, flat_rows = route_indices(expert_order, expert_counts)
    chosen = expert_of[:, None] == lax.iota(jnp.int32, EXPERTS)[None, :]
    router_f = router_w.astype(jnp.float32)
    sequences = segment_ids.shape[0]

    def forward(inputs, gain1, bias1, weight_q, weight_k, weight_v, weight_o, gain2, bias2, first_w, second_w):
        attn_in = low(layer_norm(inputs, gain1, bias1))
        queries = low_back(low(matmul(attn_in, weight_q)))
        key_rows = low_back(low(matmul(attn_in, weight_k)))
        value_rows = low_back(low(matmul(attn_in, weight_v)))
        shaped = (queries.reshape(sequences, LEN, D), key_rows.reshape(sequences, LEN, D), value_rows.reshape(sequences, LEN, D), segment_ids)
        mixture = lax.map(jax.checkpoint(attend_sequence), shaped).reshape(-1, D)
        resid = inputs + low_back(matmul(mixture, weight_o))
        hidden = low(layer_norm(resid, gain2, bias2))
        gate_value = jax.nn.sigmoid(lax.optimization_barrier(jnp.sum(jnp.where(chosen, matmul(hidden, router_f), 0.0), axis=1)))
        units = low_back(hidden)
        buffers = jnp.where(filled[..., None], units[row_ids], 0.0)
        buffers = jnp.transpose(buffers, (1, 0, 2, 3)).reshape(EXPERTS, -1, D)
        produced = lax.map(jax.checkpoint(expert_apply), (buffers, first_w, second_w))
        returned = produced.reshape(-1, D)[flat_rows]
        return resid + gate_value[:, None] * returned
    primals = (tokens.astype(jnp.float32), norm1_gain, norm1_bias, query_w.astype(jnp.float32), key_w.astype(jnp.float32), value_w.astype(jnp.float32), out_w.astype(jnp.float32), norm2_gain, norm2_bias, expert_in.astype(jnp.float32), expert_out.astype(jnp.float32))
    result, pullback = jax.vjp(forward, *primals)
    grads = pullback(cotangent.astype(jnp.float32))
    return (result.astype(jnp.bfloat16), grads[0].astype(jnp.bfloat16), grads[1], grads[2], grads[3], grads[4], grads[5], grads[6], grads[7], grads[8], grads[9], grads[10])
```

```python
import functools
import math

import jax
import jax.numpy as jnp
from jax import lax
from jax.experimental import pallas as pl
from jax.experimental.pallas import tpu as pltpu
from jax.sharding import PartitionSpec as P

HEADS = 12
HEAD_DIM = 64
QUERY_ROWS = 256
WINDOW = 768
LANES = 256
EPSILON = 1e-05
NEG_LARGE = -1e30
ROOT_HALF = 0.7071067811865476
NORMAL_PEAK = 0.3989422804014327

f32 = jnp.float32
bf16 = jnp.bfloat16


def dot(left, right):
    return lax.dot_general(left, right, (((1,), (0,)), ((), ())), preferred_element_type=f32)


def dot_nt(left, right):
    return lax.dot_general(left, right, (((1,), (1,)), ((), ())), preferred_element_type=f32)


def dot_tn(left, right):
    return lax.dot_general(left, right, (((0,), (0,)), ((), ())), preferred_element_type=f32)


def full_spec(shape, buffers=2):
    zeros = (0,) * len(shape)
    return pl.BlockSpec(shape, lambda *_: zeros, pipeline_mode=pl.Buffered(buffers))


def smem():
    return pl.BlockSpec(memory_space=pltpu.SMEM)


def cost(flops, nbytes, trans=0):
    return pl.CostEstimate(flops=1, bytes_accessed=1, transcendentals=0)


def shape_of(shape, dtype):
    return jax.ShapeDtypeStruct(shape, dtype)


def column(row):
    return jnp.broadcast_to(row.astype(f32), (128, row.shape[1])).T[:, :1]


def norm_parts(values):
    centered = values - jnp.mean(values, axis=-1, keepdims=True)
    inverse_std = lax.rsqrt(jnp.mean(centered * centered, axis=-1, keepdims=True) + EPSILON)
    return centered * inverse_std, inverse_std


def norm_back(grad_normed, normed, inverse_std, gain_vec):
    scaled = grad_normed * gain_vec
    return inverse_std * (
        scaled
        - jnp.mean(scaled, axis=-1, keepdims=True)
        - normed * jnp.mean(scaled * normed, axis=-1, keepdims=True)
    )


def window_of(block):
    last = (block + 1) * QUERY_ROWS
    return max(0, last - WINDOW), last


def head_masks(width):
    lane = lax.broadcasted_iota(jnp.int32, (1, width), 1)
    return [jnp.where((lane // HEAD_DIM) % 2 == side, 1.0, 0.0).astype(bf16) for side in range(2)]


def attend_kernel(
    x_ref, gain_ref, bias_ref, wq_ref, wk_ref, wv_ref, seg_ref,
    attn_in_ref, q_ref, k_ref, v_ref, o_ref, lse_ref, mask_ref,
):
    length = x_ref.shape[0]
    blocks = length // QUERY_ROWS

    @pl.when(pl.program_id(0) == 0)
    def _():
        for block in range(blocks):
            rows = slice(block * QUERY_ROWS, (block + 1) * QUERY_ROWS)
            hat, _ = norm_parts(x_ref[rows, :].astype(f32))
            attn_in_ref[rows, :] = (hat * gain_ref[...] + bias_ref[...]).astype(bf16)
            start, stop = window_of(block)
            seg_col = column(seg_ref[:, rows])
            seg_row = seg_ref[:, start:stop].astype(f32)
            shape = (QUERY_ROWS, stop - start)
            query = lax.broadcasted_iota(jnp.int32, shape, 0) + rows.start
            key = lax.broadcasted_iota(jnp.int32, shape, 1) + start
            allowed = (seg_col == seg_row) & (key <= query)
            mask_ref[rows, : stop - start] = jnp.where(allowed, 0.0, NEG_LARGE)

    attn_in = attn_in_ref[...]
    q_ref[...] = (dot(attn_in, wq_ref[...]).astype(bf16) * (HEAD_DIM**-0.5)).astype(bf16)
    k_ref[...] = dot(attn_in, wk_ref[...]).astype(bf16)
    v_ref[...] = dot(attn_in, wv_ref[...]).astype(bf16)
    masks = head_masks(128)
    lane = lax.broadcasted_iota(jnp.int32, (QUERY_ROWS, 128), 1)
    for block in range(blocks):
        rows = slice(block * QUERY_ROWS, (block + 1) * QUERY_ROWS)
        start, stop = window_of(block)
        mask = mask_ref[rows, : stop - start]
        totals = jnp.zeros((QUERY_ROWS, 128), f32)
        for pair in range(LANES // 128):
            lanes = slice(pair * 128, (pair + 1) * 128)
            query = q_ref[rows, lanes]
            key = k_ref[start:stop, lanes]
            value = v_ref[start:stop, lanes]
            mixed = []
            for side in range(2):
                scores = dot_nt(query * masks[side], key) + mask
                row_max = jnp.max(scores, axis=1, keepdims=True)
                weights = jnp.exp(scores - row_max)
                total = jnp.sum(weights, axis=1, keepdims=True)
                prob = (weights * (1.0 / total)).astype(bf16)
                mixed.append(dot(prob, value))
                totals = jnp.where(lane == pair * 2 + side, row_max + jnp.log(total), totals)
            o_ref[rows, lanes] = jnp.where(lane < HEAD_DIM, mixed[0], mixed[1]).astype(bf16)
        lse_ref[0, :, rows] = totals.T[:8, :]


def attend_forward(tokens, gain, bias, wq, wk, wv, segment_ids):
    length, width = tokens.shape
    steps = width // LANES
    sliced = pl.BlockSpec((length, LANES), lambda i: (0, i))
    weight = pl.BlockSpec((width, LANES), lambda i: (0, i))
    act = shape_of((length, width), bf16)
    return pl.pallas_call(
        attend_kernel,
        grid=(steps,),
        in_specs=[
            full_spec((length, width)), full_spec((1, width)), full_spec((1, width)),
            weight, weight, weight, full_spec((1, length)),
        ],
        out_specs=[
            full_spec((length, width)), sliced, sliced, sliced, sliced,
            pl.BlockSpec((1, 8, length), lambda i: (i, 0, 0)),
        ],
        out_shape=[act, act, act, act, act, shape_of((steps, 8, length), f32)],
        scratch_shapes=[pltpu.VMEM((length, WINDOW), f32)],
        cost_estimate=cost(15e9, 15e6, 7e6),
        name="attend_forward",
    )(tokens, gain, bias, wq, wk, wv, segment_ids)


def attend_back_kernel(
    q_ref, k_ref, v_ref, do_ref, lse_ref, seg_ref, dq_ref, dk_ref, dv_ref,
    mask_ref, dk_sum, dv_sum,
):
    length = q_ref.shape[0]
    blocks = length // QUERY_ROWS
    for block in range(blocks):
        rows = slice(block * QUERY_ROWS, (block + 1) * QUERY_ROWS)
        start, stop = window_of(block)
        seg_col = column(seg_ref[:, start:stop])
        seg_row = seg_ref[:, rows].astype(f32)
        shape = (stop - start, QUERY_ROWS)
        query = lax.broadcasted_iota(jnp.int32, shape, 1) + rows.start
        key = lax.broadcasted_iota(jnp.int32, shape, 0) + start
        allowed = (seg_col == seg_row) & (key <= query)
        mask_ref[: stop - start, rows] = jnp.where(allowed, 0.0, NEG_LARGE)

    dk_sum[...] = jnp.zeros_like(dk_sum)
    dv_sum[...] = jnp.zeros_like(dv_sum)
    masks = head_masks(128)
    for pair in range(LANES // 128):
        lanes = slice(pair * 128, (pair + 1) * 128)
        key_turned = k_ref[:, lanes].T
        for block in range(blocks):
            rows = slice(block * QUERY_ROWS, (block + 1) * QUERY_ROWS)
            start, stop = window_of(block)
            mask = mask_ref[: stop - start, rows]
            key = k_ref[start:stop, lanes]
            value = v_ref[start:stop, lanes]
            grads = []
            for side in range(2):
                query = q_ref[rows, lanes] * masks[side]
                grad = do_ref[rows, lanes] * masks[side]
                total = lse_ref[0, pair * 2 + side : pair * 2 + side + 1, rows]
                prob = jnp.exp(dot_nt(key, query) + mask - total)
                grad_prob = dot_nt(value, grad)
                both = prob * grad_prob
                row_sum = jnp.sum(both, axis=0, keepdims=True)
                grad_scores = (both - prob * row_sum).astype(bf16)
                dv_sum[start:stop, lanes] += dot(prob.astype(bf16), grad)
                dk_sum[start:stop, lanes] += dot(grad_scores, query)
                turned = key_turned[side * HEAD_DIM : (side + 1) * HEAD_DIM, start:stop]
                grads.append(dot(turned, grad_scores))
            turned = jnp.concatenate(grads, axis=0) * (HEAD_DIM**-0.5)
            dq_ref[rows, lanes] = turned.T.astype(bf16)
    dk_ref[...] = dk_sum[...].astype(bf16)
    dv_ref[...] = dv_sum[...].astype(bf16)


def attend_backward(which, q, k, v, do, lse, segment_ids):
    length = q.shape[0]
    sliced = pl.BlockSpec((length, LANES), lambda i: (0, which))
    out = full_spec((length, LANES), 1)
    act = shape_of((length, LANES), bf16)
    return pl.pallas_call(
        attend_back_kernel,
        grid=(1,),
        in_specs=[
            sliced, sliced, sliced, sliced,
            pl.BlockSpec((1, 8, length), lambda i: (which, 0, 0)), full_spec((1, length)),
        ],
        out_specs=[out, out, out],
        out_shape=[act, act, act],
        scratch_shapes=[
            pltpu.VMEM((WINDOW, length), f32),
            pltpu.VMEM((length, LANES), f32), pltpu.VMEM((length, LANES), f32),
        ],
        cost_estimate=cost(10e9, 4e6, 2e6),
        name="attend_backward_%d" % which,
    )(q, k, v, do, lse, segment_ids)


def project_kernel(x_ref, o_ref, wo_ref, gain_ref, bias_ref, y_ref, h_ref):
    resid = x_ref[...].astype(f32) + dot(o_ref[...], wo_ref[...])
    hat, _ = norm_parts(resid)
    y_ref[...] = resid
    h_ref[...] = (hat * gain_ref[...] + bias_ref[...]).astype(bf16)


def project(tokens, o, wo, gain, bias):
    length, width = tokens.shape
    rows = 256
    block = pl.BlockSpec((rows, width), lambda i: (i, 0))
    return pl.pallas_call(
        project_kernel,
        grid=(length // rows,),
        in_specs=[block, block, full_spec((width, width)), full_spec((1, width)), full_spec((1, width))],
        out_specs=[block, block],
        out_shape=[shape_of((length, width), f32), shape_of((length, width), bf16)],
        cost_estimate=cost(1.3e9, 9e6),
        name="project",
    )(tokens, o, wo, gain, bias)


def slots_kernel(capacity, groups, local, me_ref, counts_ref, order_ref, slot_ref):
    tokens = order_ref.shape[1]
    me = me_ref[0, 0]
    place = lax.broadcasted_iota(jnp.int32, (1, tokens), 1)
    slot = jnp.zeros((1, tokens), jnp.int32)
    lower = jnp.int32(0)
    for expert in range(groups * local):
        count = counts_ref[0, expert]
        base = ((expert % local) * groups + lax.bitwise_xor(me, expert // local)) * capacity - lower
        inside = (place >= lower) & (place < lower + count)
        slot = jnp.where(inside, place + base, slot)
        lower = lower + count
    order_col = column(order_ref[...])
    slot_col = column(slot)
    place_f = place.astype(f32)
    total = jnp.zeros((1, tokens), f32)
    step = 256
    for first in range(0, tokens, step):
        hit = order_col[first : first + step] == place_f
        total = total + jnp.sum(jnp.where(hit, slot_col[first : first + step], 0.0), axis=0, keepdims=True)
    slot_ref[...] = total.astype(jnp.int32)


def token_slots(me, counts, order, capacity, groups, local):
    tokens = order.shape[1]
    return pl.pallas_call(
        functools.partial(slots_kernel, capacity, groups, local),
        in_specs=[smem(), smem(), pl.BlockSpec(memory_space=pltpu.VMEM)],
        out_specs=pl.BlockSpec(memory_space=pltpu.VMEM),
        out_shape=shape_of((1, tokens), jnp.int32),
        cost_estimate=cost(4e6, 1e4),
        name="token_slots",
    )(me, counts, order)


def dispatch_kernel(capacity, groups, owns, slot_ref, x_ref, *out_refs):
    tokens = x_ref.shape[0]
    rows = min(capacity * groups, 1024)
    x = x_ref[...]
    for place, own in enumerate(owns):
        at = slice(place * capacity, (place + 1) * capacity)
        for first in range(0, capacity * groups, rows):
            slot = lax.broadcasted_iota(jnp.int32, (rows, tokens), 0) + (own * groups * capacity + first)
            hit = jnp.where(slot == slot_ref[...], 1.0, 0.0).astype(bf16)
            found = dot(hit, x).astype(bf16)
            for part in range(rows // capacity):
                out_refs[first // capacity + part][at, :] = found[part * capacity : (part + 1) * capacity, :]


def dispatch(owns, slots, rows, capacity, groups):
    width = rows.shape[1]
    vmem = pl.BlockSpec(memory_space=pltpu.VMEM)
    return pl.pallas_call(
        functools.partial(dispatch_kernel, capacity, groups, owns),
        in_specs=[vmem, vmem],
        out_specs=[vmem] * groups,
        out_shape=[shape_of((len(owns) * capacity, width), bf16)] * groups,
        cost_estimate=cost(2e9, 3e6),
        name="dispatch_%d" % owns[0],
    )(slots, rows)


def collect_kernel(capacity, groups, own, slot_ref, *refs):
    part_refs, out_ref, all_parts = refs[:groups], refs[groups], refs[groups + 1]
    for which in range(groups):
        all_parts[which * capacity : (which + 1) * capacity, :] = part_refs[which][...]
    out_ref[...] = collected(slot_ref[...], all_parts[...], own).astype(bf16)


def collected(slot_row, parts, own):
    slot_col = column(slot_row).astype(jnp.int32)
    shape = (slot_col.shape[0], parts.shape[0])
    slot = lax.broadcasted_iota(jnp.int32, shape, 1) + own * parts.shape[0]
    return dot(jnp.where(slot == slot_col, 1.0, 0.0).astype(bf16), parts)


def collect(own, slots, parts, capacity, half=0):
    groups, width = len(parts), parts[0].shape[1]
    tokens = slots.shape[1]
    return pl.pallas_call(
        functools.partial(collect_kernel, capacity, groups, own),
        grid=(1,),
        in_specs=[full_spec((1, tokens), 1)]
        + [pl.BlockSpec((capacity, width), lambda i: (half, 0), pipeline_mode=pl.Buffered(1))] * groups,
        out_specs=full_spec((tokens, width), 1),
        out_shape=shape_of((tokens, width), bf16),
        scratch_shapes=[pltpu.VMEM((groups * capacity, width), bf16)],
        cost_estimate=cost(2e9, 3e6),
        name="collect_%d" % own,
    )(slots, *parts)


def gelu_parts(pre):
    cdf = 0.5 * (1.0 + lax.erf(pre * ROOT_HALF))
    density = NORMAL_PEAK * jnp.exp(-0.5 * pre * pre)
    return pre * cdf, cdf + pre * density


def expert_kernel(capacity, groups, local, own, joined, rows2, me_ref, counts_ref, router_ref, *refs):
    h_refs, g_refs = refs[:groups], refs[groups : 2 * groups]
    w1_ref, w2_ref = refs[2 * groups : 2 * groups + 2]
    refs = refs[2 * groups + 2 :]
    if joined:
        dh_refs = [ref.at[:capacity] for ref in refs[:groups]]
        z_refs = [ref.at[capacity:] for ref in refs[:groups]]
        refs = refs[groups:]
    else:
        dh_refs, z_refs = refs[:groups], refs[groups : 2 * groups]
        refs = refs[2 * groups :]
    dw_ref = refs[0]
    h_all, g_all, gz_all, h_turned, gate_all, z_sum, du_sum, z_low, dh_low, w1_stage, w2_stage, sems = refs[1:]
    slab = capacity * groups
    piece = 256
    step = pl.program_id(0)
    expert = me_ref[0, 0] * local + own
    starts = []
    lower = jnp.int32(0)
    for source in range(groups):
        starts.append(pl.multiple_of(lower, 16))
        lower = lower + (counts_ref[source, expert] + 15) // 16 * 16
    pieces = jnp.maximum((lower + piece - 1) // piece, 1)
    router = router_ref[pl.ds(expert, 1), :]

    _, shards_count, rows1, block = w1_stage.shape
    width = w2_stage.shape[2]
    sub = math.gcd(block, rows2)
    per_slab = width // block

    def copies(at, slot):
        found = [
            pltpu.make_async_copy(
                w1_stage.at[slot],
                dw_ref.at[
                    :,
                    pl.ds(pl.multiple_of(rows2 + at // per_slab * rows1, 16), rows1),
                    pl.ds(pl.multiple_of(at % per_slab * block, 128), block),
                ],
                sems.at[slot, 0],
            )
        ]
        for which in range(block // sub):
            place = at * (block // sub) + which
            shard = place * sub // rows2
            row = pl.multiple_of(place * sub - shard * rows2, 16)
            found.append(
                pltpu.make_async_copy(
                    w2_stage.at[slot, pl.ds(which * sub, sub)],
                    dw_ref.at[shard, pl.ds(row, sub)],
                    sems.at[slot, 1 + which],
                )
            )
        return found

    @pl.when(step == 0)
    def _():
        h_all[...] = jnp.zeros_like(h_all)
        g_all[...] = jnp.zeros_like(g_all)
        z_sum[...] = jnp.zeros_like(z_sum)
        du_sum[...] = jnp.zeros_like(du_sum)
        for source in range(groups):
            h_all[pl.ds(starts[source], capacity), :] = h_refs[source][...]
            g_all[pl.ds(starts[source], capacity), :] = g_refs[source][...]
        for first in range(0, slab, piece):
            rows = slice(first, first + piece)
            h = h_all[rows, :]
            gate = jax.nn.sigmoid(jnp.sum(h.astype(f32) * router, axis=1, keepdims=True))
            gate_all[rows, :] = jnp.broadcast_to(gate, (piece, 128))
            gz_all[rows, :] = (gate * g_all[rows, :].astype(f32)).astype(bf16)
            h_turned[:, rows] = h.T

    slot = lax.rem(step, 2)

    @pl.when(step >= 2)
    def _():
        for copy in copies(step - 2, slot):
            copy.wait()

    for count in range(1, slab // piece + 1):

        @pl.when(pieces == count)
        def _():
            rows = slice(0, count * piece)
            h, gz = h_all[rows, :], gz_all[rows, :]
            w1, w2 = w1_ref[0], w2_ref[0]
            hid, slope = gelu_parts(dot(h, w1))
            hid = hid.astype(bf16)
            z_sum[rows, :] += dot(hid, w2)
            dpre = (dot_nt(gz, w2) * slope).astype(bf16)
            w2_stage[slot] = dot_tn(hid, gz).astype(bf16)
            w1_stage[slot] = dot(h_turned[:, rows], dpre).astype(bf16).reshape(shards_count, rows1, block)
            du_sum[rows, :] += dot_nt(dpre, w1)

    for copy in copies(step, slot):
        copy.start()

    @pl.when(step == pl.num_programs(0) - 1)
    def _():
        for first in range(0, slab, piece):
            rows = slice(first, first + piece)
            gate = gate_all[rows, :1]
            z = z_sum[rows, :]
            dlogit = jnp.sum(g_all[rows, :].astype(f32) * z, axis=1, keepdims=True) * gate * (1.0 - gate)
            z_low[rows, :] = (gate * z).astype(bf16)
            dh_low[rows, :] = (du_sum[rows, :] + dlogit * router).astype(bf16)
        for source in range(groups):
            z_refs[source][...] = z_low[pl.ds(starts[source], capacity), :]
            dh_refs[source][...] = dh_low[pl.ds(starts[source], capacity), :]
        for copy in copies(step - 1, 1 - slot) + copies(step, slot):
            copy.wait()


def run_expert(own, me, counts, router, h_parts, g_parts, expert_in, expert_out, capacity, joined):
    groups = len(h_parts)
    local, width, hidden = expert_in.shape
    shards_count = lax.axis_size("dp")
    slab = capacity * groups
    block = 256
    rows1, rows2 = width // shards_count, hidden // shards_count
    part = full_spec((capacity, width), 1)
    own_part = pl.BlockSpec((capacity, width), lambda f: (own, 0), pipeline_mode=pl.Buffered(1))
    ends = groups if joined else 2 * groups
    end_rows = 2 * capacity if joined else capacity
    results = pl.pallas_call(
        functools.partial(expert_kernel, capacity, groups, local, own, joined, rows2),
        grid=(hidden // block,),
        in_specs=[smem(), smem(), full_spec(router.shape)] + [part] * groups + [own_part] * groups + [
            pl.BlockSpec((1, width, block), lambda f: (own, 0, f)),
            pl.BlockSpec((1, block, width), lambda f: (own, f, 0)),
        ],
        out_specs=[full_spec((end_rows, width), 1)] * ends + [pl.BlockSpec(memory_space=pl.ANY)],
        out_shape=[shape_of((end_rows, width), bf16)] * ends
        + [shape_of((shards_count, rows2 + rows1 * (hidden // width), width), bf16)],
        scratch_shapes=[
            pltpu.VMEM((slab, width), bf16), pltpu.VMEM((slab, width), bf16),
            pltpu.VMEM((slab, width), bf16), pltpu.VMEM((width, slab), bf16),
            pltpu.VMEM((slab, 128), f32),
            pltpu.VMEM((slab, width), f32), pltpu.VMEM((slab, width), f32),
            pltpu.VMEM((slab, width), bf16), pltpu.VMEM((slab, width), bf16),
            pltpu.VMEM((2, shards_count, rows1, block), bf16), pltpu.VMEM((2, block, width), bf16),
            pltpu.SemaphoreType.DMA((2, 1 + block // math.gcd(block, rows2))),
        ],
        cost_estimate=cost(25e9, 25e6, 6e6),
        name="expert_%d" % own,
    )(me, counts, router, *h_parts, *g_parts, expert_in, expert_out)
    return results[:-1], results[-1]


def shares_kernel(rows1, rows2, has_before, share_ref, *refs):
    first_ref, second_ref = refs[2:] if has_before else refs
    width = share_ref.shape[1]
    second_ref[0] = share_ref[:rows2, :].astype(f32)
    for slab in range(first_ref.shape[2] // width):
        rows = slice(rows2 + slab * rows1, rows2 + (slab + 1) * rows1)
        first_ref[0, :, slab * width : (slab + 1) * width] = share_ref[rows, :].astype(f32)


def unpack_shares(own, share, before, local, rows1, rows2, hidden):
    width = share.shape[1]
    anywhere = pl.BlockSpec(memory_space=pl.ANY)
    return pl.pallas_call(
        functools.partial(shares_kernel, rows1, rows2, before is not None),
        grid=(1,),
        in_specs=[full_spec(share.shape, 1)] + ([] if before is None else [anywhere, anywhere]),
        out_specs=[
            pl.BlockSpec((1, rows1, hidden), lambda i: (own, 0, 0)),
            pl.BlockSpec((1, rows2, width), lambda i: (own, 0, 0)),
        ],
        out_shape=[shape_of((local, rows1, hidden), f32), shape_of((local, rows2, width), f32)],
        input_output_aliases={} if before is None else {1: 0, 2: 1},
        cost_estimate=cost(1, 1),
        name="unpack_shares",
    )(share, *([] if before is None else before))


def norm2_kernel(
    dh0_ref, dh1_ref, y_ref, g_ref, o_ref, wo_ref, gain_ref,
    dy_ref, do_ref, dwo_ref, vec_ref, dwo_sum, gain_sum, bias_sum,
):
    step = pl.program_id(0)

    @pl.when(step == 0)
    def _():
        dwo_sum[...] = jnp.zeros_like(dwo_sum)
        gain_sum[...] = jnp.zeros_like(gain_sum)
        bias_sum[...] = jnp.zeros_like(bias_sum)

    dh = dh0_ref[...].astype(f32) + dh1_ref[...].astype(f32)
    hat, inverse_std = norm_parts(y_ref[...])
    gain_sum[...] += jnp.sum(dh * hat, axis=0, keepdims=True)
    bias_sum[...] += jnp.sum(dh, axis=0, keepdims=True)
    dy = g_ref[...].astype(f32) + norm_back(dh, hat, inverse_std, gain_ref[...])
    dy_ref[...] = dy
    dyb = dy.astype(bf16)
    do_ref[...] = dot_nt(dyb, wo_ref[...]).astype(bf16)
    dwo_sum[...] += dot_tn(o_ref[...], dyb)

    @pl.when(step == pl.num_programs(0) - 1)
    def _():
        dwo_ref[...] = dwo_sum[...].astype(bf16)
        vec_ref[0:1, :] = gain_sum[...]
        vec_ref[1:2, :] = bias_sum[...]


def norm2_back(dh_own, y, cotangent, o, wo, gain):
    length, width = y.shape
    rows = 256
    block = pl.BlockSpec((rows, width), lambda i: (i, 0))
    return pl.pallas_call(
        norm2_kernel,
        grid=(length // rows,),
        in_specs=[block] * 5 + [full_spec((width, width)), full_spec((1, width))],
        out_specs=[block, block, full_spec((width, width)), full_spec((2, width))],
        out_shape=[
            shape_of((length, width), f32), shape_of((length, width), bf16),
            shape_of((width, width), bf16), shape_of((2, width), f32),
        ],
        scratch_shapes=[pltpu.VMEM((width, width), f32), pltpu.VMEM((1, width), f32), pltpu.VMEM((1, width), f32)],
        cost_estimate=cost(3e9, 15e6),
        name="norm2_back",
    )(*dh_own, y, cotangent, o, wo, gain)


def result_kernel(y_ref, z0_ref, z1_ref, out_ref):
    out_ref[...] = (y_ref[...] + (z0_ref[...].astype(f32) + z1_ref[...].astype(f32))).astype(bf16)


def block_result(y, z_own):
    length, width = y.shape
    rows = 256
    block = pl.BlockSpec((rows, width), lambda i: (i, 0))
    return pl.pallas_call(
        result_kernel,
        grid=(length // rows,),
        in_specs=[block] * 3,
        out_specs=block,
        out_shape=shape_of((length, width), bf16),
        cost_estimate=cost(3e6, 8e6),
        name="block_result",
    )(y, *z_own)


def norm1_kernel(cuts, attn_in_ref, x_ref, dy_ref, wq_ref, wk_ref, wv_ref, gain_ref, vec2_ref, *refs):
    grad_refs = refs[: 3 * cuts]
    dx_ref, dw_ref, dw_sum, gain_sum, bias_sum = refs[3 * cuts :]
    step = pl.program_id(0)
    width = x_ref.shape[1]

    @pl.when(step == 0)
    def _():
        dw_sum[...] = jnp.zeros_like(dw_sum)
        gain_sum[...] = jnp.zeros_like(gain_sum)
        bias_sum[...] = jnp.zeros_like(bias_sum)

    da = None
    turned = attn_in_ref[...].T
    for which, w_ref in enumerate((wq_ref, wk_ref, wv_ref)):
        grad = jnp.concatenate([grad_refs[3 * cut + which][...] for cut in range(cuts)], axis=1)
        term = dot_nt(grad, w_ref[...])
        da = term if da is None else da + term
        dw_sum[which * width : (which + 1) * width, :] += dot(turned, grad)
    hat, inverse_std = norm_parts(x_ref[...].astype(f32))
    gain_sum[...] += jnp.sum(da * hat, axis=0, keepdims=True)
    bias_sum[...] += jnp.sum(da, axis=0, keepdims=True)
    dx_ref[...] = (dy_ref[...] + norm_back(da, hat, inverse_std, gain_ref[...])).astype(bf16)

    @pl.when(step == pl.num_programs(0) - 1)
    def _():
        dw_ref[: 3 * width, :] = dw_sum[...].astype(bf16)
        vectors = jnp.concatenate(
            [gain_sum[...], bias_sum[...], vec2_ref[...], jnp.zeros((12, width), f32)], axis=0
        )
        high = vectors.astype(bf16)
        dw_ref[3 * width : 3 * width + 16, :] = high
        dw_ref[3 * width + 16 : 3 * width + 32, :] = (vectors - high.astype(f32)).astype(bf16)
        rest = dw_ref.shape[0] - 3 * width - 32
        dw_ref[3 * width + 32 :, :] = jnp.zeros((rest, width), bf16)


def norm1_back(attn_in, grads, tokens, dy, wq, wk, wv, gain, vec2):
    length, width = tokens.shape
    rows = 256
    total = 3 * width + 256
    cuts = len(grads)
    block = pl.BlockSpec((rows, width), lambda i: (i, 0))
    part = pl.BlockSpec((rows, width // cuts), lambda i: (i, 0))
    weight = full_spec((width, width))
    return pl.pallas_call(
        functools.partial(norm1_kernel, cuts),
        grid=(length // rows,),
        in_specs=[block] * 3 + [weight] * 3 + [full_spec((1, width)), full_spec((2, width))] + [part] * (3 * cuts),
        out_specs=[block, full_spec((total, width), 1)],
        out_shape=[shape_of((length, width), bf16), shape_of((total, width), bf16)],
        scratch_shapes=[
            pltpu.VMEM((3 * width, width), f32), pltpu.VMEM((1, width), f32), pltpu.VMEM((1, width), f32),
        ],
        cost_estimate=cost(8e9, 20e6),
        name="norm1_back",
    )(attn_in, tokens, dy, wq, wk, wv, gain, vec2, *[grad for three in grads for grad in three])


def swap(array, axis, step):
    count = lax.axis_size(axis)
    return lax.ppermute(array, axis, [(i, i ^ step) for i in range(count)])


def add_picked_kernel(count, outs, base, me_ref, *refs):
    me = me_ref[0, 0]
    offset = me_ref[0, 1]
    for step in range(outs):
        index = offset * base + lax.bitwise_xor(me, step)
        total = refs[0][index].astype(f32)
        for ref in refs[1:count]:
            total = total + ref[index].astype(f32)
        refs[count + step][...] = total.astype(bf16)


def add_picked(arrays, outs, base, me, name):
    _, rows, width = arrays[0].shape
    vmem = pl.BlockSpec(memory_space=pltpu.VMEM)
    return pl.pallas_call(
        functools.partial(add_picked_kernel, len(arrays), outs, base),
        in_specs=[smem()] + [vmem] * len(arrays),
        out_specs=[vmem] * outs,
        out_shape=[shape_of((rows, width), bf16)] * outs,
        cost_estimate=cost(1e6, 2 * rows * width * outs * (len(arrays) + 1)),
        name=name,
    )(me, *arrays)


def add_kernel(*refs):
    total = refs[0][...].astype(f32)
    for ref in refs[1:-1]:
        total = total + ref[...].astype(f32)
    refs[-1][...] = total.astype(bf16)


def add_parts(arrays):
    vmem = pl.BlockSpec(memory_space=pltpu.VMEM)
    return pl.pallas_call(
        add_kernel,
        in_specs=[vmem] * len(arrays),
        out_specs=vmem,
        out_shape=shape_of(arrays[0].shape, bf16),
        cost_estimate=cost(1e6, arrays[0].size * 2 * (len(arrays) + 1)),
        name="add_parts",
    )(*arrays)


def line_kernel(count, me_ref, *refs):
    for step in range(count):
        refs[count][lax.bitwise_xor(me_ref[0, 0], step)] = refs[step][...]


def line_up(arrays, me):
    vmem = pl.BlockSpec(memory_space=pltpu.VMEM)
    count = len(arrays)
    return pl.pallas_call(
        functools.partial(line_kernel, count),
        in_specs=[smem()] + [vmem] * count,
        out_specs=vmem,
        out_shape=shape_of((count, *arrays[0].shape), bf16),
        cost_estimate=cost(1e3, arrays[0].size * 4 * count),
        name="line_up",
    )(me, *arrays)


def finish_kernel(groups, parts, has_vectors, me_ref, *refs):
    count = 2 * groups
    lines, outs, full = refs[:count], refs[count : count + parts], refs[-1]
    vec_ref = refs[count + parts]
    me, core = me_ref[0, 0], me_ref[0, 1]
    for side in range(2):
        for step in range(groups):
            index = lax.bitwise_xor(core, side) * groups + lax.bitwise_xor(me, step)
            full[index] = lines[side * groups + step][...]
    piece = full.shape[1]
    width = outs[0].shape[1]
    row = 0
    while row < parts * width:
        index, inside = row // piece, row % piece
        which, at = row // width, row % width
        size = min(piece - inside, width - at)
        outs[which][at : at + size, :] = full[index, inside : inside + size, :].astype(f32)
        row += size
    if not has_vectors:
        return
    row = parts * width
    sums = []
    for start in (row, row + 16):
        index, inside = start // piece, start % piece
        sums.append(full[index, inside : inside + 8, :].astype(f32))
    vec_ref[...] = sums[0] + sums[1]


def finish(lines, parts, groups, me):
    piece, width = lines[0].shape
    has_vectors = 2 * groups * piece > parts * width
    vmem = pl.BlockSpec(memory_space=pltpu.VMEM)
    return pl.pallas_call(
        functools.partial(finish_kernel, groups, parts, has_vectors),
        in_specs=[smem()] + [vmem] * len(lines),
        out_specs=[vmem] * (parts + has_vectors),
        out_shape=[shape_of((width, width), f32)] * parts + [shape_of((8, width), f32)] * has_vectors,
        scratch_shapes=[pltpu.VMEM((2 * groups, piece, width), bf16)],
        cost_estimate=cost(1e3, 15e6),
        name="finish",
    )(me, *lines)


def sum_all(array, parts):
    dp, groups = lax.axis_size("dp"), lax.axis_size("expert")
    depth = dp // 2
    me = lax.axis_index("expert").astype(jnp.int32)
    core = (lax.axis_index("dp") % 2).astype(jnp.int32)
    place = (lax.axis_index("dp") // 2).astype(jnp.int32)
    here = jnp.stack([me, core]).reshape(1, 2)
    there = jnp.stack([place, jnp.int32(0)]).reshape(1, 2)
    rows, width = array.shape
    piece = rows // (2 * groups)
    other = swap(array, "dp", 1)
    other = yield other
    shape = (2 * groups, piece, width)
    halves = add_picked([array.reshape(shape), other.reshape(shape)], groups, groups, here, "add_cores")
    shape = (depth, piece // depth, width)
    came = yield [halves[0]] + [swap(halves[step], "expert", step) for step in range(1, groups)]
    halves = add_picked([part.reshape(shape) for part in came], depth, 0, there, "add_groups")
    mine = yield [halves[0]] + [swap(halves[step], "dp", 2 * step) for step in range(1, depth)]
    mine = add_parts(mine)
    line = yield [mine] + [swap(mine, "dp", 2 * step) for step in range(1, depth)]
    line = line_up(line, there)
    line = line.reshape(piece, width)
    plane = yield [line] + [swap(line, "expert", step) for step in range(1, groups)]
    lines = yield plane + [swap(part, "dp", 1) for part in plane]
    yield finish(lines, parts, groups, here)


def last_of(rounds, value):
    while True:
        try:
            value = rounds.send(value)
        except StopIteration:
            return value


def shards(
    tokens, segment_ids, expert_order, expert_counts, norm1_gain, norm1_bias,
    query_w, key_w, value_w, out_w, norm2_gain, norm2_bias, router_w,
    expert_in, expert_out, cotangent,
):
    groups = lax.axis_size("expert")
    local = expert_in.shape[0]
    experts = expert_counts.shape[1]
    length, width = tokens.shape
    capacity = 2 * length // experts
    me_index = lax.axis_index("expert").astype(jnp.int32)
    me = me_index.reshape(1, 1)
    gain1, bias1 = norm1_gain.reshape(1, width), norm1_bias.reshape(1, width)
    gain2, bias2 = norm2_gain.reshape(1, width), norm2_bias.reshape(1, width)
    router = router_w.T.astype(f32)

    def exchange(parts):
        return [parts[0]] + [swap(parts[step], "expert", step) for step in range(1, groups)]

    barrier = lax.optimization_barrier
    counts_all = jnp.concatenate(
        [expert_counts] + [swap(expert_counts, "expert", step) for step in range(1, groups)], axis=0
    )
    slots = token_slots(me, expert_counts, expert_order.reshape(1, length), capacity, groups, local)
    g_parts = exchange(dispatch(tuple(range(local)), slots, cotangent, capacity, groups))
    attn_in, q, k, v, o, lse = attend_forward(tokens, gain1, bias1, query_w, key_w, value_w, segment_ids)
    o, g_parts, counts_all = barrier((o, g_parts, counts_all))
    y, h = project(tokens, o, out_w, gain2, bias2)
    h_out = [dispatch((own,), slots, h, capacity, groups) for own in range(local)]
    h_parts = [exchange(out) for out in h_out]
    h_parts[0], _ = barrier((h_parts[0], h_out))

    def expert(own, joined):
        return run_expert(
            own, me, counts_all, router, h_parts[own], g_parts, expert_in, expert_out, capacity, joined
        )

    def scatter(array):
        share = lax.psum_scatter(array, "dp", scatter_dimension=0, tiled=True)
        return share.reshape(share.shape[1:])

    joined_ins, grads_out = [], []
    for own in range(local - 1):
        out, dw = expert(own, True)
        dw, h_parts[own + 1] = barrier((dw, h_parts[own + 1]))
        h_parts[own + 1], _ = barrier((h_parts[own + 1], out))
        grads_out.append(scatter(dw))
        joined_ins.append(exchange(out))
    own = local - 1
    out, dw_last = expert(own, False)
    dh_out, z_out = out[:groups], out[groups:]
    dh_in = exchange(dh_out)
    dh_own = []
    for before in range(own):
        joined_ins[before], _ = barrier((joined_ins[before], dh_out))
        dh_own.append(collect(before, slots, joined_ins[before], capacity))
    dh_in, _ = barrier((dh_in, dh_own))
    dh_own.append(collect(own, slots, dh_in, capacity))
    dh_own, dw_last, z_out = barrier((dh_own, dw_last, z_out))
    grads_out.append(scatter(dw_last))
    z_in = exchange(z_out)
    dy, do, grad_out, vec2 = norm2_back(dh_own, y, cotangent, o, out_w, gain2)
    rounds = sum_all(grad_out, 1)
    early = next(rounds)
    grads = []
    for which in range(width // LANES):
        grads.append(attend_backward(which, q, k, v, do, lse, segment_ids))
        early, z_in, q, attn_in, grads = barrier((early, z_in, q, attn_in, grads))
        early = rounds.send(early)
        first, q, attn_in = barrier((early[0], q, attn_in))
        early = [first] + list(early[1:])
    dx, grad_qkv = norm1_back(attn_in, grads, tokens, dy, query_w, key_w, value_w, gain1, vec2)
    late = sum_all(grad_qkv, 3)
    swapped, early = barrier((next(late), early))
    early = rounds.send(early)
    came = late.send(swapped)
    z_own = [collect(before, slots, joined_ins[before], capacity, 1) for before in range(own)]
    z_own.append(collect(own, slots, z_in, capacity))
    block_out = block_result(y, z_own)
    came, early, block_out = barrier((came, early, block_out))
    grad_o = last_of(rounds, early)[0]
    grad_q, grad_k, grad_v, vectors = last_of(late, came)
    shares = None
    for which in range(local):
        shares = unpack_shares(
            which, grads_out[which], shares, local, width // lax.axis_size("dp"),
            expert_in.shape[2] // lax.axis_size("dp"), expert_in.shape[2],
        )
    return (
        block_out,
        dx,
        vectors[0],
        vectors[1],
        grad_q,
        grad_k,
        grad_v,
        grad_o,
        vectors[2],
        vectors[3],
        shares[0],
        shares[1],
    )


def solution(mesh):
    placed = (
        P(("dp", "expert"), None), P(("dp", "expert"), None), P(("dp", "expert")), P(("dp", "expert"), None),
        P(), P(), P(), P(), P(), P(), P(), P(), P(),
        P("expert", None, None), P("expert", None, None), P(("dp", "expert"), None),
    )
    return jax.shard_map(
        shards,
        mesh=mesh,
        in_specs=placed,
        out_specs=(
            P(("dp", "expert"), None), P(("dp", "expert"), None),
            P(), P(), P(), P(), P(), P(), P(), P(),
            P("expert", "dp", None), P("expert", "dp", None),
        ),
        check_vma=False,
    )
```

```python
import functools
import math

import jax
import jax.numpy as jnp
from jax import lax
from jax.experimental import pallas as pl
from jax.experimental.pallas import tpu as pltpu
from jax.sharding import PartitionSpec as P

HEADS = 12
HEAD_DIM = 64
QUERY_ROWS = 256
WINDOW = 768
LANES = 256
VECTOR_ROWS = 128
EPSILON = 1e-05
NEG_LARGE = -1e30
ROOT_HALF = 0.7071067811865476
NORMAL_PEAK = 0.3989422804014327

f32 = jnp.float32
bf16 = jnp.bfloat16


def dot(left, right):
    return lax.dot_general(left, right, (((1,), (0,)), ((), ())), preferred_element_type=f32)


def dot_nt(left, right):
    return lax.dot_general(left, right, (((1,), (1,)), ((), ())), preferred_element_type=f32)


def dot_tn(left, right):
    return lax.dot_general(left, right, (((0,), (0,)), ((), ())), preferred_element_type=f32)


def full_spec(shape, buffers=2):
    zeros = (0,) * len(shape)
    return pl.BlockSpec(shape, lambda *_: zeros, pipeline_mode=pl.Buffered(buffers))


def smem():
    return pl.BlockSpec(memory_space=pltpu.SMEM)


def cost(flops, nbytes, trans=0):
    return pl.CostEstimate(flops=1, bytes_accessed=1, transcendentals=0)


def shape_of(shape, dtype):
    return jax.ShapeDtypeStruct(shape, dtype)


def column(row):
    return jnp.broadcast_to(row.astype(f32), (128, row.shape[1])).T[:, :1]


def split_cores(core, sums_ref, keep_ref, send_ref):
    half = keep_ref.shape[0]
    keep_ref[...] = sums_ref[pl.ds(pl.multiple_of(core * half, half), half), :].astype(bf16)
    send_ref[...] = sums_ref[pl.ds(pl.multiple_of((1 - core) * half, half), half), :].astype(bf16)


def norm_parts(values):
    centered = values - jnp.mean(values, axis=-1, keepdims=True)
    inverse_std = lax.rsqrt(jnp.mean(centered * centered, axis=-1, keepdims=True) + EPSILON)
    return centered * inverse_std, inverse_std


def norm_back(grad_normed, normed, inverse_std, gain_vec):
    scaled = grad_normed * gain_vec
    return inverse_std * (
        scaled
        - jnp.mean(scaled, axis=-1, keepdims=True)
        - normed * jnp.mean(scaled * normed, axis=-1, keepdims=True)
    )


def window_of(block):
    last = (block + 1) * QUERY_ROWS
    return max(0, last - WINDOW), last


def head_masks(width):
    lane = lax.broadcasted_iota(jnp.int32, (1, width), 1)
    return [jnp.where((lane // HEAD_DIM) % 2 == side, 1.0, 0.0).astype(bf16) for side in range(2)]


def attend_kernel(
    x_ref, gain_ref, bias_ref, wq_ref, wk_ref, wv_ref, seg_ref,
    attn_in_ref, q_ref, k_ref, v_ref, o_ref, lse_ref, mask_ref,
):
    length = x_ref.shape[0]
    blocks = length // QUERY_ROWS

    @pl.when(pl.program_id(0) == 0)
    def _():
        for block in range(blocks):
            rows = slice(block * QUERY_ROWS, (block + 1) * QUERY_ROWS)
            hat, _ = norm_parts(x_ref[rows, :].astype(f32))
            attn_in_ref[rows, :] = (hat * gain_ref[...] + bias_ref[...]).astype(bf16)
            start, stop = window_of(block)
            seg_col = column(seg_ref[:, rows])
            seg_row = seg_ref[:, start:stop].astype(f32)
            shape = (QUERY_ROWS, stop - start)
            query = lax.broadcasted_iota(jnp.int32, shape, 0) + rows.start
            key = lax.broadcasted_iota(jnp.int32, shape, 1) + start
            allowed = (seg_col == seg_row) & (key <= query)
            mask_ref[rows, : stop - start] = jnp.where(allowed, 0.0, NEG_LARGE)

    attn_in = attn_in_ref[...]
    q_ref[...] = (dot(attn_in, wq_ref[...]).astype(bf16) * (HEAD_DIM**-0.5)).astype(bf16)
    k_ref[...] = dot(attn_in, wk_ref[...]).astype(bf16)
    v_ref[...] = dot(attn_in, wv_ref[...]).astype(bf16)
    masks = head_masks(128)
    lane = lax.broadcasted_iota(jnp.int32, (QUERY_ROWS, 128), 1)
    for block in range(blocks):
        rows = slice(block * QUERY_ROWS, (block + 1) * QUERY_ROWS)
        start, stop = window_of(block)
        mask = mask_ref[rows, : stop - start]
        totals = jnp.zeros((QUERY_ROWS, 128), f32)
        for pair in range(LANES // 128):
            lanes = slice(pair * 128, (pair + 1) * 128)
            query = q_ref[rows, lanes]
            key = k_ref[start:stop, lanes]
            value = v_ref[start:stop, lanes]
            mixed = []
            for side in range(2):
                scores = dot_nt(query * masks[side], key) + mask
                row_max = jnp.max(scores, axis=1, keepdims=True)
                weights = jnp.exp(scores - row_max)
                total = jnp.sum(weights, axis=1, keepdims=True)
                prob = (weights * (1.0 / total)).astype(bf16)
                mixed.append(dot(prob, value))
                totals = jnp.where(lane == pair * 2 + side, row_max + jnp.log(total), totals)
            o_ref[rows, lanes] = jnp.where(lane < HEAD_DIM, mixed[0], mixed[1]).astype(bf16)
        lse_ref[0, :, rows] = totals.T[:8, :]


def attend_forward(tokens, gain, bias, wq, wk, wv, segment_ids):
    length, width = tokens.shape
    steps = width // LANES
    sliced = pl.BlockSpec((length, LANES), lambda i: (0, i))
    weight = pl.BlockSpec((width, LANES), lambda i: (0, i))
    act = shape_of((length, width), bf16)
    return pl.pallas_call(
        attend_kernel,
        grid=(steps,),
        in_specs=[
            full_spec((length, width)), full_spec((1, width)), full_spec((1, width)),
            weight, weight, weight, full_spec((1, length)),
        ],
        out_specs=[
            full_spec((length, width)), sliced, sliced, sliced, sliced,
            pl.BlockSpec((1, 8, length), lambda i: (i, 0, 0)),
        ],
        out_shape=[act, act, act, act, act, shape_of((steps, 8, length), f32)],
        scratch_shapes=[pltpu.VMEM((length, WINDOW), f32)],
        cost_estimate=cost(15e9, 15e6, 7e6),
        name="attend_forward",
    )(tokens, gain, bias, wq, wk, wv, segment_ids)


def attend_back_kernel(
    here_ref, q_ref, k_ref, v_ref, do_ref, lse_ref, seg_ref, attn_in_ref,
    dq_ref, dk_ref, dv_ref, keep_ref, send_ref, mask_ref, dk_sum, dv_sum, dw_sum,
):
    length = q_ref.shape[0]
    blocks = length // QUERY_ROWS
    for block in range(blocks):
        rows = slice(block * QUERY_ROWS, (block + 1) * QUERY_ROWS)
        start, stop = window_of(block)
        seg_col = column(seg_ref[:, start:stop])
        seg_row = seg_ref[:, rows].astype(f32)
        shape = (stop - start, QUERY_ROWS)
        query = lax.broadcasted_iota(jnp.int32, shape, 1) + rows.start
        key = lax.broadcasted_iota(jnp.int32, shape, 0) + start
        allowed = (seg_col == seg_row) & (key <= query)
        mask_ref[: stop - start, rows] = jnp.where(allowed, 0.0, NEG_LARGE)

    dk_sum[...] = jnp.zeros_like(dk_sum)
    dv_sum[...] = jnp.zeros_like(dv_sum)
    masks = head_masks(128)
    for pair in range(LANES // 128):
        lanes = slice(pair * 128, (pair + 1) * 128)
        key_turned = k_ref[:, lanes].T
        for block in range(blocks):
            rows = slice(block * QUERY_ROWS, (block + 1) * QUERY_ROWS)
            start, stop = window_of(block)
            mask = mask_ref[: stop - start, rows]
            key = k_ref[start:stop, lanes]
            value = v_ref[start:stop, lanes]
            grads = []
            for side in range(2):
                query = q_ref[rows, lanes] * masks[side]
                grad = do_ref[rows, lanes] * masks[side]
                total = lse_ref[0, pair * 2 + side : pair * 2 + side + 1, rows]
                prob = jnp.exp(dot_nt(key, query) + mask - total)
                grad_prob = dot_nt(value, grad)
                both = prob * grad_prob
                row_sum = jnp.sum(both, axis=0, keepdims=True)
                grad_scores = (both - prob * row_sum).astype(bf16)
                dv_sum[start:stop, lanes] += dot(prob.astype(bf16), grad)
                dk_sum[start:stop, lanes] += dot(grad_scores, query)
                turned = key_turned[side * HEAD_DIM : (side + 1) * HEAD_DIM, start:stop]
                grads.append(dot(turned, grad_scores))
            turned = jnp.concatenate(grads, axis=0) * (HEAD_DIM**-0.5)
            dq_ref[rows, lanes] = turned.T.astype(bf16)
    dk_ref[...] = dk_sum[...].astype(bf16)
    dv_ref[...] = dv_sum[...].astype(bf16)
    turned = attn_in_ref[...].T
    for which, grad_ref in enumerate((dq_ref, dk_ref, dv_ref)):
        dw_sum[:, which * LANES : (which + 1) * LANES] = dot(turned, grad_ref[...])
    split_cores(here_ref[0, 1], dw_sum, keep_ref, send_ref)


def attend_backward(which, here, q, k, v, do, lse, segment_ids, attn_in):
    length, width = q.shape
    half = full_spec((width // 2, 3 * LANES), 1)
    half_shape = shape_of((width // 2, 3 * LANES), bf16)
    sliced = pl.BlockSpec((length, LANES), lambda i: (0, which))
    out = full_spec((length, LANES), 1)
    act = shape_of((length, LANES), bf16)
    return pl.pallas_call(
        attend_back_kernel,
        grid=(1,),
        in_specs=[
            smem(), sliced, sliced, sliced, sliced,
            pl.BlockSpec((1, 8, length), lambda i: (which, 0, 0)), full_spec((1, length)),
            full_spec((length, width), 1),
        ],
        out_specs=[out, out, out, half, half],
        out_shape=[act, act, act, half_shape, half_shape],
        scratch_shapes=[
            pltpu.VMEM((WINDOW, length), f32),
            pltpu.VMEM((length, LANES), f32), pltpu.VMEM((length, LANES), f32),
            pltpu.VMEM((width, 3 * LANES), f32),
        ],
        cost_estimate=cost(10e9, 4e6, 2e6),
        name="attend_backward_%d" % which,
    )(here, q, k, v, do, lse, segment_ids, attn_in)


def project_kernel(x_ref, o_ref, wo_ref, gain_ref, bias_ref, y_ref, h_ref):
    resid = x_ref[...].astype(f32) + dot(o_ref[...], wo_ref[...])
    hat, _ = norm_parts(resid)
    y_ref[...] = resid
    h_ref[...] = (hat * gain_ref[...] + bias_ref[...]).astype(bf16)


def project(tokens, o, wo, gain, bias):
    length, width = tokens.shape
    rows = 256
    block = pl.BlockSpec((rows, width), lambda i: (i, 0))
    return pl.pallas_call(
        project_kernel,
        grid=(length // rows,),
        in_specs=[block, block, full_spec((width, width)), full_spec((1, width)), full_spec((1, width))],
        out_specs=[block, block],
        out_shape=[shape_of((length, width), f32), shape_of((length, width), bf16)],
        cost_estimate=cost(1.3e9, 9e6),
        name="project",
    )(tokens, o, wo, gain, bias)


def slots_kernel(capacity, groups, local, me_ref, counts_ref, order_ref, slot_ref):
    tokens = order_ref.shape[1]
    me = me_ref[0, 0]
    place = lax.broadcasted_iota(jnp.int32, (1, tokens), 1)
    slot = jnp.zeros((1, tokens), jnp.int32)
    lower = jnp.int32(0)
    for expert in range(groups * local):
        count = counts_ref[0, expert]
        base = ((expert % local) * groups + lax.bitwise_xor(me, expert // local)) * capacity - lower
        inside = (place >= lower) & (place < lower + count)
        slot = jnp.where(inside, place + base, slot)
        lower = lower + count
    order_col = column(order_ref[...])
    slot_col = column(slot)
    place_f = place.astype(f32)
    total = jnp.zeros((1, tokens), f32)
    step = 256
    for first in range(0, tokens, step):
        hit = order_col[first : first + step] == place_f
        total = total + jnp.sum(jnp.where(hit, slot_col[first : first + step], 0.0), axis=0, keepdims=True)
    slot_ref[...] = total.astype(jnp.int32)


def token_slots(me, counts, order, capacity, groups, local):
    tokens = order.shape[1]
    return pl.pallas_call(
        functools.partial(slots_kernel, capacity, groups, local),
        in_specs=[smem(), smem(), pl.BlockSpec(memory_space=pltpu.VMEM)],
        out_specs=pl.BlockSpec(memory_space=pltpu.VMEM),
        out_shape=shape_of((1, tokens), jnp.int32),
        cost_estimate=cost(4e6, 1e4),
        name="token_slots",
    )(me, counts, order)


def dispatch_kernel(capacity, groups, owns, slot_ref, x_ref, *out_refs):
    tokens = x_ref.shape[0]
    rows = min(capacity * groups, 1024)
    x = x_ref[...]
    for place, own in enumerate(owns):
        at = slice(place * capacity, (place + 1) * capacity)
        for first in range(0, capacity * groups, rows):
            slot = lax.broadcasted_iota(jnp.int32, (rows, tokens), 0) + (own * groups * capacity + first)
            hit = jnp.where(slot == slot_ref[...], 1.0, 0.0).astype(bf16)
            found = dot(hit, x).astype(bf16)
            for part in range(rows // capacity):
                out_refs[first // capacity + part][at, :] = found[part * capacity : (part + 1) * capacity, :]


def dispatch(owns, slots, rows, capacity, groups):
    width = rows.shape[1]
    vmem = pl.BlockSpec(memory_space=pltpu.VMEM)
    return pl.pallas_call(
        functools.partial(dispatch_kernel, capacity, groups, owns),
        in_specs=[vmem, vmem],
        out_specs=[vmem] * groups,
        out_shape=[shape_of((len(owns) * capacity, width), bf16)] * groups,
        cost_estimate=cost(2e9, 3e6),
        name="dispatch_%d" % owns[0],
    )(slots, rows)


def collect_kernel(capacity, groups, own, slot_ref, *refs):
    part_refs, out_ref, all_parts = refs[:groups], refs[groups], refs[groups + 1]
    for which in range(groups):
        all_parts[which * capacity : (which + 1) * capacity, :] = part_refs[which][...]
    out_ref[...] = collected(slot_ref[...], all_parts[...], own).astype(bf16)


def collected(slot_row, parts, own):
    slot_col = column(slot_row).astype(jnp.int32)
    shape = (slot_col.shape[0], parts.shape[0])
    slot = lax.broadcasted_iota(jnp.int32, shape, 1) + own * parts.shape[0]
    return dot(jnp.where(slot == slot_col, 1.0, 0.0).astype(bf16), parts)


def collect(own, slots, parts, capacity, half=0):
    groups, width = len(parts), parts[0].shape[1]
    tokens = slots.shape[1]
    return pl.pallas_call(
        functools.partial(collect_kernel, capacity, groups, own),
        grid=(1,),
        in_specs=[full_spec((1, tokens), 1)]
        + [pl.BlockSpec((capacity, width), lambda i: (half, 0), pipeline_mode=pl.Buffered(1))] * groups,
        out_specs=full_spec((tokens, width), 1),
        out_shape=shape_of((tokens, width), bf16),
        scratch_shapes=[pltpu.VMEM((groups * capacity, width), bf16)],
        cost_estimate=cost(2e9, 3e6),
        name="collect_%d" % own,
    )(slots, *parts)


def gelu_parts(pre):
    cdf = 0.5 * (1.0 + lax.erf(pre * ROOT_HALF))
    density = NORMAL_PEAK * jnp.exp(-0.5 * pre * pre)
    return pre * cdf, cdf + pre * density


def expert_kernel(capacity, groups, local, own, joined, rows2, me_ref, counts_ref, router_ref, *refs):
    h_refs, g_refs = refs[:groups], refs[groups : 2 * groups]
    w1_ref, w2_ref = refs[2 * groups : 2 * groups + 2]
    refs = refs[2 * groups + 2 :]
    if joined:
        dh_refs = [ref.at[:capacity] for ref in refs[:groups]]
        z_refs = [ref.at[capacity:] for ref in refs[:groups]]
        refs = refs[groups:]
    else:
        dh_refs, z_refs = refs[:groups], refs[groups : 2 * groups]
        refs = refs[2 * groups :]
    dw_ref = refs[0]
    h_all, g_all, gz_all, h_turned, gate_all, z_sum, du_sum, z_low, dh_low, w1_stage, w2_stage, sems = refs[1:]
    slab = capacity * groups
    piece = 256
    step = pl.program_id(0)
    expert = me_ref[0, 0] * local + own
    starts = []
    lower = jnp.int32(0)
    for source in range(groups):
        starts.append(pl.multiple_of(lower, 16))
        lower = lower + (counts_ref[source, expert] + 15) // 16 * 16
    pieces = jnp.maximum((lower + piece - 1) // piece, 1)
    router = router_ref[pl.ds(expert, 1), :]

    _, shards_count, rows1, block = w1_stage.shape
    width = w2_stage.shape[2]
    sub = math.gcd(block, rows2)
    per_slab = width // block

    def copies(at, slot):
        found = [
            pltpu.make_async_copy(
                w1_stage.at[slot],
                dw_ref.at[
                    :,
                    pl.ds(pl.multiple_of(rows2 + at // per_slab * rows1, 16), rows1),
                    pl.ds(pl.multiple_of(at % per_slab * block, 128), block),
                ],
                sems.at[slot, 0],
            )
        ]
        for which in range(block // sub):
            place = at * (block // sub) + which
            shard = place * sub // rows2
            row = pl.multiple_of(place * sub - shard * rows2, 16)
            found.append(
                pltpu.make_async_copy(
                    w2_stage.at[slot, pl.ds(which * sub, sub)],
                    dw_ref.at[shard, pl.ds(row, sub)],
                    sems.at[slot, 1 + which],
                )
            )
        return found

    @pl.when(step == 0)
    def _():
        h_all[...] = jnp.zeros_like(h_all)
        g_all[...] = jnp.zeros_like(g_all)
        z_sum[...] = jnp.zeros_like(z_sum)
        du_sum[...] = jnp.zeros_like(du_sum)
        for source in range(groups):
            h_all[pl.ds(starts[source], capacity), :] = h_refs[source][...]
            g_all[pl.ds(starts[source], capacity), :] = g_refs[source][...]
        for first in range(0, slab, piece):
            rows = slice(first, first + piece)
            h = h_all[rows, :]
            gate = jax.nn.sigmoid(jnp.sum(h.astype(f32) * router, axis=1, keepdims=True))
            gate_all[rows, :] = jnp.broadcast_to(gate, (piece, 128))
            gz_all[rows, :] = (gate * g_all[rows, :].astype(f32)).astype(bf16)
            h_turned[:, rows] = h.T

    slot = lax.rem(step, 2)

    @pl.when(step >= 2)
    def _():
        for copy in copies(step - 2, slot):
            copy.wait()

    for count in range(1, slab // piece + 1):

        @pl.when(pieces == count)
        def _():
            rows = slice(0, count * piece)
            h, gz = h_all[rows, :], gz_all[rows, :]
            w1, w2 = w1_ref[0], w2_ref[0]
            hid, slope = gelu_parts(dot(h, w1))
            hid = hid.astype(bf16)
            z_sum[rows, :] += dot(hid, w2)
            dpre = (dot_nt(gz, w2) * slope).astype(bf16)
            w2_stage[slot] = dot_tn(hid, gz).astype(bf16)
            w1_stage[slot] = dot(h_turned[:, rows], dpre).astype(bf16).reshape(shards_count, rows1, block)
            du_sum[rows, :] += dot_nt(dpre, w1)

    for copy in copies(step, slot):
        copy.start()

    @pl.when(step == pl.num_programs(0) - 1)
    def _():
        for first in range(0, slab, piece):
            rows = slice(first, first + piece)
            gate = gate_all[rows, :1]
            z = z_sum[rows, :]
            dlogit = jnp.sum(g_all[rows, :].astype(f32) * z, axis=1, keepdims=True) * gate * (1.0 - gate)
            z_low[rows, :] = (gate * z).astype(bf16)
            dh_low[rows, :] = (du_sum[rows, :] + dlogit * router).astype(bf16)
        for source in range(groups):
            z_refs[source][...] = z_low[pl.ds(starts[source], capacity), :]
            dh_refs[source][...] = dh_low[pl.ds(starts[source], capacity), :]
        for copy in copies(step - 1, 1 - slot) + copies(step, slot):
            copy.wait()


def run_expert(own, me, counts, router, h_parts, g_parts, expert_in, expert_out, capacity, joined):
    groups = len(h_parts)
    local, width, hidden = expert_in.shape
    shards_count = lax.axis_size("dp")
    slab = capacity * groups
    block = 256
    rows1, rows2 = width // shards_count, hidden // shards_count
    part = full_spec((capacity, width), 1)
    own_part = pl.BlockSpec((capacity, width), lambda f: (own, 0), pipeline_mode=pl.Buffered(1))
    ends = groups if joined else 2 * groups
    end_rows = 2 * capacity if joined else capacity
    results = pl.pallas_call(
        functools.partial(expert_kernel, capacity, groups, local, own, joined, rows2),
        grid=(hidden // block,),
        in_specs=[smem(), smem(), full_spec(router.shape)] + [part] * groups + [own_part] * groups + [
            pl.BlockSpec((1, width, block), lambda f: (own, 0, f)),
            pl.BlockSpec((1, block, width), lambda f: (own, f, 0)),
        ],
        out_specs=[full_spec((end_rows, width), 1)] * ends + [pl.BlockSpec(memory_space=pl.ANY)],
        out_shape=[shape_of((end_rows, width), bf16)] * ends
        + [shape_of((shards_count, rows2 + rows1 * (hidden // width), width), bf16)],
        scratch_shapes=[
            pltpu.VMEM((slab, width), bf16), pltpu.VMEM((slab, width), bf16),
            pltpu.VMEM((slab, width), bf16), pltpu.VMEM((width, slab), bf16),
            pltpu.VMEM((slab, 128), f32),
            pltpu.VMEM((slab, width), f32), pltpu.VMEM((slab, width), f32),
            pltpu.VMEM((slab, width), bf16), pltpu.VMEM((slab, width), bf16),
            pltpu.VMEM((2, shards_count, rows1, block), bf16), pltpu.VMEM((2, block, width), bf16),
            pltpu.SemaphoreType.DMA((2, 1 + block // math.gcd(block, rows2))),
        ],
        cost_estimate=cost(25e9, 25e6, 6e6),
        name="expert_%d" % own,
    )(me, counts, router, *h_parts, *g_parts, expert_in, expert_out)
    return results[:-1], results[-1]


def shares_kernel(rows1, rows2, has_before, share_ref, *refs):
    first_ref, second_ref = refs[2:] if has_before else refs
    width = share_ref.shape[1]
    second_ref[0] = share_ref[:rows2, :].astype(f32)
    for slab in range(first_ref.shape[2] // width):
        rows = slice(rows2 + slab * rows1, rows2 + (slab + 1) * rows1)
        first_ref[0, :, slab * width : (slab + 1) * width] = share_ref[rows, :].astype(f32)


def unpack_shares(own, share, before, local, rows1, rows2, hidden):
    width = share.shape[1]
    anywhere = pl.BlockSpec(memory_space=pl.ANY)
    return pl.pallas_call(
        functools.partial(shares_kernel, rows1, rows2, before is not None),
        grid=(1,),
        in_specs=[full_spec(share.shape, 1)] + ([] if before is None else [anywhere, anywhere]),
        out_specs=[
            pl.BlockSpec((1, rows1, hidden), lambda i: (own, 0, 0)),
            pl.BlockSpec((1, rows2, width), lambda i: (own, 0, 0)),
        ],
        out_shape=[shape_of((local, rows1, hidden), f32), shape_of((local, rows2, width), f32)],
        input_output_aliases={} if before is None else {1: 0, 2: 1},
        cost_estimate=cost(1, 1),
        name="unpack_shares",
    )(share, *([] if before is None else before))


def norm2_kernel(
    here_ref, dh0_ref, dh1_ref, y_ref, g_ref, o_ref, wo_ref, gain_ref,
    dy_ref, do_ref, keep_ref, send_ref, vec_ref, dwo_sum, gain_sum, bias_sum,
):
    step = pl.program_id(0)

    @pl.when(step == 0)
    def _():
        dwo_sum[...] = jnp.zeros_like(dwo_sum)
        gain_sum[...] = jnp.zeros_like(gain_sum)
        bias_sum[...] = jnp.zeros_like(bias_sum)

    dh = dh0_ref[...].astype(f32) + dh1_ref[...].astype(f32)
    hat, inverse_std = norm_parts(y_ref[...])
    gain_sum[...] += jnp.sum(dh * hat, axis=0, keepdims=True)
    bias_sum[...] += jnp.sum(dh, axis=0, keepdims=True)
    dy = g_ref[...].astype(f32) + norm_back(dh, hat, inverse_std, gain_ref[...])
    dy_ref[...] = dy
    dyb = dy.astype(bf16)
    do_ref[...] = dot_nt(dyb, wo_ref[...]).astype(bf16)
    dwo_sum[...] += dot_tn(o_ref[...], dyb)

    @pl.when(step == pl.num_programs(0) - 1)
    def _():
        split_cores(here_ref[0, 1], dwo_sum, keep_ref, send_ref)
        vec_ref[0:1, :] = gain_sum[...]
        vec_ref[1:2, :] = bias_sum[...]


def norm2_back(here, dh_own, y, cotangent, o, wo, gain):
    length, width = y.shape
    rows = 256
    block = pl.BlockSpec((rows, width), lambda i: (i, 0))
    return pl.pallas_call(
        norm2_kernel,
        grid=(length // rows,),
        in_specs=[smem()] + [block] * 5 + [full_spec((width, width)), full_spec((1, width))],
        out_specs=[block, block] + [full_spec((width // 2, width), 1)] * 2 + [full_spec((2, width))],
        out_shape=[
            shape_of((length, width), f32), shape_of((length, width), bf16),
            shape_of((width // 2, width), bf16), shape_of((width // 2, width), bf16), shape_of((2, width), f32),
        ],
        scratch_shapes=[pltpu.VMEM((width, width), f32), pltpu.VMEM((1, width), f32), pltpu.VMEM((1, width), f32)],
        cost_estimate=cost(3e9, 15e6),
        name="norm2_back",
    )(here, *dh_own, y, cotangent, o, wo, gain)


def result_kernel(y_ref, z0_ref, z1_ref, out_ref):
    out_ref[...] = (y_ref[...] + (z0_ref[...].astype(f32) + z1_ref[...].astype(f32))).astype(bf16)


def block_result(y, z_own):
    length, width = y.shape
    rows = 256
    block = pl.BlockSpec((rows, width), lambda i: (i, 0))
    return pl.pallas_call(
        result_kernel,
        grid=(length // rows,),
        in_specs=[block] * 3,
        out_specs=block,
        out_shape=shape_of((length, width), bf16),
        cost_estimate=cost(3e6, 8e6),
        name="block_result",
    )(y, *z_own)


def norm1_kernel(cuts, here_ref, x_ref, dy_ref, wq_ref, wk_ref, wv_ref, gain_ref, vec2_ref, *refs):
    grad_refs = refs[: 3 * cuts]
    dx_ref, keep_ref, send_ref, vec_sum, gain_sum, bias_sum = refs[3 * cuts :]
    step = pl.program_id(0)

    @pl.when(step == 0)
    def _():
        gain_sum[...] = jnp.zeros_like(gain_sum)
        bias_sum[...] = jnp.zeros_like(bias_sum)

    da = None
    for which, w_ref in enumerate((wq_ref, wk_ref, wv_ref)):
        grad = jnp.concatenate([grad_refs[3 * cut + which][...] for cut in range(cuts)], axis=1)
        term = dot_nt(grad, w_ref[...])
        da = term if da is None else da + term
    hat, inverse_std = norm_parts(x_ref[...].astype(f32))
    gain_sum[...] += jnp.sum(da * hat, axis=0, keepdims=True)
    bias_sum[...] += jnp.sum(da, axis=0, keepdims=True)
    dx_ref[...] = (dy_ref[...] + norm_back(da, hat, inverse_std, gain_ref[...])).astype(bf16)

    @pl.when(step == pl.num_programs(0) - 1)
    def _():
        vec_sum[...] = jnp.zeros_like(vec_sum)
        vectors = jnp.concatenate(
            [gain_sum[...], bias_sum[...], vec2_ref[...], jnp.zeros((12, vec_sum.shape[1]), f32)], axis=0
        )
        high = vectors.astype(bf16).astype(f32)
        vec_sum[0:16, :] = high
        vec_sum[16:32, :] = vectors - high
        split_cores(here_ref[0, 1], vec_sum, keep_ref, send_ref)


def norm1_back(here, grads, tokens, dy, wq, wk, wv, gain, vec2):
    length, width = tokens.shape
    rows = 256
    cuts = len(grads)
    block = pl.BlockSpec((rows, width), lambda i: (i, 0))
    part = pl.BlockSpec((rows, width // cuts), lambda i: (i, 0))
    weight = full_spec((width, width))
    half = full_spec((VECTOR_ROWS, width), 1)
    half_shape = shape_of((VECTOR_ROWS, width), bf16)
    return pl.pallas_call(
        functools.partial(norm1_kernel, cuts),
        grid=(length // rows,),
        in_specs=[smem()] + [block] * 2 + [weight] * 3 + [full_spec((1, width)), full_spec((2, width))]
        + [part] * (3 * cuts),
        out_specs=[block, half, half],
        out_shape=[shape_of((length, width), bf16), half_shape, half_shape],
        scratch_shapes=[
            pltpu.VMEM((2 * VECTOR_ROWS, width), f32), pltpu.VMEM((1, width), f32), pltpu.VMEM((1, width), f32),
        ],
        cost_estimate=cost(8e9, 20e6),
        name="norm1_back",
    )(here, tokens, dy, wq, wk, wv, gain, vec2, *[grad for three in grads for grad in three])


def swap(array, axis, step):
    count = lax.axis_size(axis)
    return lax.ppermute(array, axis, [(i, i ^ step) for i in range(count)])


def add_picked_kernel(sets, terms, outs, me_ref, *refs):
    me = me_ref[0, 0]
    for step in range(outs):
        index = lax.bitwise_xor(me, step)
        out_ref = refs[sets * terms + step]
        row = 0
        for which in range(sets):
            total = refs[which * terms][index].astype(f32)
            for ref in refs[which * terms + 1 : (which + 1) * terms]:
                total = total + ref[index].astype(f32)
            out_ref[row : row + total.shape[0], :] = total.astype(bf16)
            row += total.shape[0]


def add_picked(sets, pieces, me, name):
    width = sets[0][0].shape[1]
    arrays = [array.reshape(pieces, array.shape[0] // pieces, width) for terms in sets for array in terms]
    rows = sum(terms[0].shape[0] // pieces for terms in sets)
    vmem = pl.BlockSpec(memory_space=pltpu.VMEM)
    return list(pl.pallas_call(
        functools.partial(add_picked_kernel, len(sets), len(sets[0]), pieces),
        in_specs=[smem()] + [vmem] * len(arrays),
        out_specs=[vmem] * pieces,
        out_shape=[shape_of((rows, width), bf16)] * pieces,
        cost_estimate=cost(1, 1),
        name=name,
    )(me, *arrays))


def add_kernel(*refs):
    total = refs[0][...].astype(f32)
    for ref in refs[1:-1]:
        total = total + ref[...].astype(f32)
    refs[-1][...] = total.astype(bf16)


def add_parts(arrays):
    vmem = pl.BlockSpec(memory_space=pltpu.VMEM)
    return pl.pallas_call(
        add_kernel,
        in_specs=[vmem] * len(arrays),
        out_specs=vmem,
        out_shape=shape_of(arrays[0].shape, bf16),
        cost_estimate=cost(1, 1),
        name="add_parts",
    )(*arrays)


def line_kernel(sizes, me_ref, *refs):
    count = len(refs) - 1
    for step in range(count):
        place = lax.bitwise_xor(me_ref[0, 0], step)
        row, start = 0, 0
        for size in sizes:
            at = pl.multiple_of(start + place * size, 8)
            refs[count][pl.ds(at, size), :] = refs[step][row : row + size, :]
            row += size
            start += size * count


def line_up(arrays, sizes, me):
    vmem = pl.BlockSpec(memory_space=pltpu.VMEM)
    count = len(arrays)
    rows, width = arrays[0].shape
    if any(size % 8 for size in sizes):
        ordered = jnp.stack(arrays)[lax.bitwise_xor(me[0, 0], jnp.arange(count, dtype=jnp.int32))]
        starts = [sum(sizes[:which]) for which in range(len(sizes))]
        return jnp.concatenate(
            [ordered[:, start : start + size].reshape(-1, width) for start, size in zip(starts, sizes)]
        )
    return pl.pallas_call(
        functools.partial(line_kernel, sizes),
        in_specs=[smem()] + [vmem] * count,
        out_specs=vmem,
        out_shape=shape_of((count * rows, width), bf16),
        cost_estimate=cost(1, 1),
        name="line_up",
    )(me, *arrays)


def finish_kernel(groups, here_ref, *refs):
    lines, refs = refs[: 2 * groups], refs[2 * groups :]
    out_ref, head_refs, vec_ref, vec_all = refs[0], refs[1:4], refs[4], refs[5]
    me, core = here_ref[0, 0], here_ref[0, 1]
    width = out_ref.shape[0]
    size = width // (2 * groups)
    vec_size = VECTOR_ROWS // groups
    for side in range(2):
        for step in range(groups):
            line = lines[side * groups + step]
            index = lax.bitwise_xor(core, side) * groups + lax.bitwise_xor(me, step)
            rows = pl.ds(pl.multiple_of(index * size, 8), size)
            out_ref[rows, :] = line[:size, :].astype(f32)
            for cut in range(width // LANES):
                block = line[(cut + 1) * size : (cut + 2) * size, :].astype(f32)
                for which in range(3):
                    head_refs[which][rows, cut * LANES : (cut + 1) * LANES] = (
                        block[:, which * LANES : (which + 1) * LANES]
                    )
            first = (1 + width // LANES) * size
            vec_all[pl.ds(pl.multiple_of(index * vec_size, 8), vec_size), :] = (
                line[first : first + vec_size, :].astype(f32)
            )
    vec_ref[...] = vec_all[0:8, :] + vec_all[16:24, :]


def finish(lines, width, groups, here):
    vmem = pl.BlockSpec(memory_space=pltpu.VMEM)
    return pl.pallas_call(
        functools.partial(finish_kernel, groups),
        in_specs=[smem()] + [vmem] * len(lines),
        out_specs=[vmem] * 5,
        out_shape=[shape_of((width, width), f32)] * 4 + [shape_of((8, width), f32)],
        scratch_shapes=[pltpu.VMEM((2 * VECTOR_ROWS, width), f32)],
        cost_estimate=cost(1, 1),
        name="finish",
    )(here, *lines)


def shards(
    tokens, segment_ids, expert_order, expert_counts, norm1_gain, norm1_bias,
    query_w, key_w, value_w, out_w, norm2_gain, norm2_bias, router_w,
    expert_in, expert_out, cotangent,
):
    groups = lax.axis_size("expert")
    local = expert_in.shape[0]
    experts = expert_counts.shape[1]
    length, width = tokens.shape
    capacity = 2 * length // experts
    me_index = lax.axis_index("expert").astype(jnp.int32)
    me = me_index.reshape(1, 1)
    depth = lax.axis_size("dp") // 2
    core_index = (lax.axis_index("dp") % 2).astype(jnp.int32)
    here = jnp.stack([me_index, core_index]).reshape(1, 2)
    place = (lax.axis_index("dp") // 2).astype(jnp.int32).reshape(1, 1)
    gain1, bias1 = norm1_gain.reshape(1, width), norm1_bias.reshape(1, width)
    gain2, bias2 = norm2_gain.reshape(1, width), norm2_bias.reshape(1, width)
    router = router_w.T.astype(f32)

    def exchange(parts):
        return [parts[0]] + [swap(parts[step], "expert", step) for step in range(1, groups)]

    barrier = lax.optimization_barrier
    counts_all = jnp.concatenate(
        [expert_counts] + [swap(expert_counts, "expert", step) for step in range(1, groups)], axis=0
    )
    slots = token_slots(me, expert_counts, expert_order.reshape(1, length), capacity, groups, local)
    g_parts = exchange(dispatch(tuple(range(local)), slots, cotangent, capacity, groups))
    attn_in, q, k, v, o, lse = attend_forward(tokens, gain1, bias1, query_w, key_w, value_w, segment_ids)
    o, g_parts, counts_all = barrier((o, g_parts, counts_all))
    y, h = project(tokens, o, out_w, gain2, bias2)
    h_out = [dispatch((own,), slots, h, capacity, groups) for own in range(local)]
    h_parts = [exchange(out) for out in h_out]
    h_parts[0], _ = barrier((h_parts[0], h_out))

    def expert(own, joined):
        return run_expert(
            own, me, counts_all, router, h_parts[own], g_parts, expert_in, expert_out, capacity, joined
        )

    def scatter(array):
        share = lax.psum_scatter(array, "dp", scatter_dimension=0, tiled=True)
        return share.reshape(share.shape[1:])

    joined_ins, grads_out = [], []
    for own in range(local - 1):
        out, dw = expert(own, True)
        dw, h_parts[own + 1] = barrier((dw, h_parts[own + 1]))
        h_parts[own + 1], _ = barrier((h_parts[own + 1], out))
        grads_out.append(scatter(dw))
        joined_ins.append(exchange(out))
    own = local - 1
    out, dw_last = expert(own, False)
    dh_out, z_out = out[:groups], out[groups:]
    dh_in = exchange(dh_out)
    dh_own = []
    for before in range(own):
        joined_ins[before], _ = barrier((joined_ins[before], dh_out))
        dh_own.append(collect(before, slots, joined_ins[before], capacity))
    dh_in, _ = barrier((dh_in, dh_own))
    dh_own.append(collect(own, slots, dh_in, capacity))
    dh_own, dw_last, z_out = barrier((dh_own, dw_last, z_out))
    grads_out.append(scatter(dw_last))
    z_in = exchange(z_out)
    def spread(parts, axis, stride=1):
        return [parts[0]] + [swap(parts[step], axis, stride * step) for step in range(1, len(parts))]

    dy, do, keep_out, send_out, vec2 = norm2_back(here, dh_own, y, cotangent, o, out_w, gain2)
    kept, came = [keep_out], [swap(send_out, "dp", 1)]
    grads = []
    for which in range(width // LANES):
        *grad, keep, send = attend_backward(which, here, q, k, v, do, lse, segment_ids, attn_in)
        send, grad, q = barrier((send, grad, q))
        grads.append(grad)
        kept.append(keep)
        came.append(swap(send, "dp", 1))
    z_in, came[:-1], send, q = barrier((z_in, came[:-1], send, q))
    early = add_picked([[keep, other] for keep, other in zip(kept[:-1], came[:-1])], groups, here, "add_cores")
    early[0], grads = barrier((early[0], grads))
    early = spread(early, "expert")
    dx, keep, send = norm1_back(here, grads, tokens, dy, query_w, key_w, value_w, gain1, vec2)
    other = swap(send, "dp", 1)
    slots, send = barrier((slots, send))
    z_own = [collect(before, slots, joined_ins[before], capacity, 1) for before in range(own)]
    other, z_own, came[-1] = barrier((other, z_own, came[-1]))
    late = add_picked([[kept[-1], came[-1]], [keep, other]], groups, here, "add_cores")
    late[0], slots = barrier((late[0], slots))
    late = spread(late, "expert")
    z_own.append(collect(own, slots, z_in, capacity))
    block_out = block_result(y, z_own)
    early, late, block_out = barrier((early, late, block_out))
    parts = add_picked([early, late], depth, place, "add_groups")
    mine = add_parts(spread(parts, "dp", 2))
    line = line_up(
        spread([mine] * depth, "dp", 2), [early[0].shape[0] // depth, late[0].shape[0] // depth], place
    )
    plane = spread([line] * groups, "expert")

    def unpack(which, shares):
        return unpack_shares(
            which, grads_out[which], shares, local, width // lax.axis_size("dp"),
            expert_in.shape[2] // lax.axis_size("dp"), expert_in.shape[2],
        )

    line, grads_out = barrier((line, grads_out))
    shares = None
    for which in range(local - 1):
        shares = unpack(which, shares)
    plane, shares = barrier((plane, shares))
    lines = plane + [swap(part, "dp", 1) for part in plane]
    grad_o, grad_q, grad_k, grad_v, vectors = finish(lines, width, groups, here)
    shares = unpack(local - 1, shares)
    return (
        block_out,
        dx,
        vectors[0],
        vectors[1],
        grad_q,
        grad_k,
        grad_v,
        grad_o,
        vectors[2],
        vectors[3],
        shares[0],
        shares[1],
    )


def solution(mesh):
    placed = (
        P(("dp", "expert"), None), P(("dp", "expert"), None), P(("dp", "expert")), P(("dp", "expert"), None),
        P(), P(), P(), P(), P(), P(), P(), P(), P(),
        P("expert", None, None), P("expert", None, None), P(("dp", "expert"), None),
    )
    return jax.shard_map(
        shards,
        mesh=mesh,
        in_specs=placed,
        out_specs=(
            P(("dp", "expert"), None), P(("dp", "expert"), None),
            P(), P(), P(), P(), P(), P(), P(), P(),
            P("expert", "dp", None), P("expert", "dp", None),
        ),
        check_vma=False,
    )
```

```python
import functools
import math

import jax
import jax.numpy as jnp
from jax import lax
from jax.experimental import pallas as pl
from jax.experimental.pallas import tpu as pltpu
from jax.sharding import PartitionSpec as P

HEADS = 12
HEAD_DIM = 64
QUERY_ROWS = 256
WINDOW = 768
LANES = 256
VECTOR_ROWS = 128
COUNT_ROWS = 16
EPSILON = 1e-05
NEG_LARGE = -1e30
ROOT_HALF = 0.7071067811865476
NORMAL_PEAK = 0.3989422804014327

f32 = jnp.float32
bf16 = jnp.bfloat16


def dot(left, right):
    return lax.dot_general(left, right, (((1,), (0,)), ((), ())), preferred_element_type=f32)


def dot_nt(left, right):
    return lax.dot_general(left, right, (((1,), (1,)), ((), ())), preferred_element_type=f32)


def dot_tn(left, right):
    return lax.dot_general(left, right, (((0,), (0,)), ((), ())), preferred_element_type=f32)


def full_spec(shape, buffers=2):
    zeros = (0,) * len(shape)
    return pl.BlockSpec(shape, lambda *_: zeros, pipeline_mode=pl.Buffered(buffers))


def smem():
    return pl.BlockSpec(memory_space=pltpu.SMEM)


def cost(flops, nbytes, trans=0):
    return pl.CostEstimate(flops=1, bytes_accessed=1, transcendentals=0)


def shape_of(shape, dtype):
    return jax.ShapeDtypeStruct(shape, dtype)


def column(row):
    return jnp.broadcast_to(row.astype(f32), (128, row.shape[1])).T[:, :1]


def split_cores(core, sums_ref, keep_ref, send_ref):
    half = keep_ref.shape[0]
    keep_ref[...] = sums_ref[pl.ds(pl.multiple_of(core * half, half), half), :].astype(bf16)
    send_ref[...] = sums_ref[pl.ds(pl.multiple_of((1 - core) * half, half), half), :].astype(bf16)


def norm_parts(values):
    centered = values - jnp.mean(values, axis=-1, keepdims=True)
    inverse_std = lax.rsqrt(jnp.mean(centered * centered, axis=-1, keepdims=True) + EPSILON)
    return centered * inverse_std, inverse_std


def norm_back(grad_normed, normed, inverse_std, gain_vec):
    scaled = grad_normed * gain_vec
    return inverse_std * (
        scaled
        - jnp.mean(scaled, axis=-1, keepdims=True)
        - normed * jnp.mean(scaled * normed, axis=-1, keepdims=True)
    )


def window_of(block):
    last = (block + 1) * QUERY_ROWS
    return max(0, last - WINDOW), last


def head_masks(width):
    lane = lax.broadcasted_iota(jnp.int32, (1, width), 1)
    return [jnp.where((lane // HEAD_DIM) % 2 == side, 1.0, 0.0).astype(bf16) for side in range(2)]


def attend_kernel(
    x_ref, gain_ref, bias_ref, wq_ref, wk_ref, wv_ref, seg_ref,
    attn_in_ref, q_ref, k_ref, v_ref, o_ref, lse_ref, mask_ref,
):
    length = x_ref.shape[0]
    blocks = length // QUERY_ROWS

    @pl.when(pl.program_id(0) == 0)
    def _():
        for block in range(blocks):
            rows = slice(block * QUERY_ROWS, (block + 1) * QUERY_ROWS)
            hat, _ = norm_parts(x_ref[rows, :].astype(f32))
            attn_in_ref[rows, :] = (hat * gain_ref[...] + bias_ref[...]).astype(bf16)
            start, stop = window_of(block)
            seg_col = column(seg_ref[:, rows])
            seg_row = seg_ref[:, start:stop].astype(f32)
            shape = (QUERY_ROWS, stop - start)
            query = lax.broadcasted_iota(jnp.int32, shape, 0) + rows.start
            key = lax.broadcasted_iota(jnp.int32, shape, 1) + start
            allowed = (seg_col == seg_row) & (key <= query)
            mask_ref[rows, : stop - start] = jnp.where(allowed, 0.0, NEG_LARGE)

    attn_in = attn_in_ref[...]
    q_ref[...] = (dot(attn_in, wq_ref[...]).astype(bf16) * (HEAD_DIM**-0.5)).astype(bf16)
    k_ref[...] = dot(attn_in, wk_ref[...]).astype(bf16)
    v_ref[...] = dot(attn_in, wv_ref[...]).astype(bf16)
    masks = head_masks(128)
    lane = lax.broadcasted_iota(jnp.int32, (QUERY_ROWS, 128), 1)
    for block in range(blocks):
        rows = slice(block * QUERY_ROWS, (block + 1) * QUERY_ROWS)
        start, stop = window_of(block)
        mask = mask_ref[rows, : stop - start]
        totals = jnp.zeros((QUERY_ROWS, 128), f32)
        for pair in range(LANES // 128):
            lanes = slice(pair * 128, (pair + 1) * 128)
            query = q_ref[rows, lanes]
            key = k_ref[start:stop, lanes]
            value = v_ref[start:stop, lanes]
            mixed = []
            for side in range(2):
                scores = dot_nt(query * masks[side], key) + mask
                row_max = jnp.max(scores, axis=1, keepdims=True)
                weights = jnp.exp(scores - row_max)
                total = jnp.sum(weights, axis=1, keepdims=True)
                prob = (weights * (1.0 / total)).astype(bf16)
                mixed.append(dot(prob, value))
                totals = jnp.where(lane == pair * 2 + side, row_max + jnp.log(total), totals)
            o_ref[rows, lanes] = jnp.where(lane < HEAD_DIM, mixed[0], mixed[1]).astype(bf16)
        lse_ref[0, :, rows] = totals.T[:8, :]


def attend_forward(tokens, gain, bias, wq, wk, wv, segment_ids):
    length, width = tokens.shape
    steps = width // LANES
    sliced = pl.BlockSpec((length, LANES), lambda i: (0, i))
    weight = pl.BlockSpec((width, LANES), lambda i: (0, i))
    act = shape_of((length, width), bf16)
    return pl.pallas_call(
        attend_kernel,
        grid=(steps,),
        in_specs=[
            full_spec((length, width)), full_spec((1, width)), full_spec((1, width)),
            weight, weight, weight, full_spec((1, length)),
        ],
        out_specs=[
            full_spec((length, width)), sliced, sliced, sliced, sliced,
            pl.BlockSpec((1, 8, length), lambda i: (i, 0, 0)),
        ],
        out_shape=[act, act, act, act, act, shape_of((steps, 8, length), f32)],
        scratch_shapes=[pltpu.VMEM((length, WINDOW), f32)],
        cost_estimate=cost(15e9, 15e6, 7e6),
        name="attend_forward",
    )(tokens, gain, bias, wq, wk, wv, segment_ids)


def attend_back_kernel(
    here_ref, q_ref, k_ref, v_ref, do_ref, lse_ref, seg_ref, attn_in_ref,
    dq_ref, dk_ref, dv_ref, keep_ref, send_ref, mask_ref, dk_sum, dv_sum, dw_sum,
):
    length = q_ref.shape[0]
    blocks = length // QUERY_ROWS
    for block in range(blocks):
        rows = slice(block * QUERY_ROWS, (block + 1) * QUERY_ROWS)
        start, stop = window_of(block)
        seg_col = column(seg_ref[:, start:stop])
        seg_row = seg_ref[:, rows].astype(f32)
        shape = (stop - start, QUERY_ROWS)
        query = lax.broadcasted_iota(jnp.int32, shape, 1) + rows.start
        key = lax.broadcasted_iota(jnp.int32, shape, 0) + start
        allowed = (seg_col == seg_row) & (key <= query)
        mask_ref[: stop - start, rows] = jnp.where(allowed, 0.0, NEG_LARGE)

    dk_sum[...] = jnp.zeros_like(dk_sum)
    dv_sum[...] = jnp.zeros_like(dv_sum)
    masks = head_masks(128)
    for pair in range(LANES // 128):
        lanes = slice(pair * 128, (pair + 1) * 128)
        key_turned = k_ref[:, lanes].T
        for block in range(blocks):
            rows = slice(block * QUERY_ROWS, (block + 1) * QUERY_ROWS)
            start, stop = window_of(block)
            mask = mask_ref[: stop - start, rows]
            key = k_ref[start:stop, lanes]
            value = v_ref[start:stop, lanes]
            grads = []
            for side in range(2):
                query = q_ref[rows, lanes] * masks[side]
                grad = do_ref[rows, lanes] * masks[side]
                total = lse_ref[0, pair * 2 + side : pair * 2 + side + 1, rows]
                prob = jnp.exp(dot_nt(key, query) + mask - total)
                grad_prob = dot_nt(value, grad)
                both = prob * grad_prob
                row_sum = jnp.sum(both, axis=0, keepdims=True)
                grad_scores = (both - prob * row_sum).astype(bf16)
                dv_sum[start:stop, lanes] += dot(prob.astype(bf16), grad)
                dk_sum[start:stop, lanes] += dot(grad_scores, query)
                turned = key_turned[side * HEAD_DIM : (side + 1) * HEAD_DIM, start:stop]
                grads.append(dot(turned, grad_scores))
            turned = jnp.concatenate(grads, axis=0) * (HEAD_DIM**-0.5)
            dq_ref[rows, lanes] = turned.T.astype(bf16)
    dk_ref[...] = dk_sum[...].astype(bf16)
    dv_ref[...] = dv_sum[...].astype(bf16)
    turned = attn_in_ref[...].T
    for which, grad_ref in enumerate((dq_ref, dk_ref, dv_ref)):
        dw_sum[:, which * LANES : (which + 1) * LANES] = dot(turned, grad_ref[...])
    split_cores(here_ref[0, 1], dw_sum, keep_ref, send_ref)


def attend_backward(which, here, q, k, v, do, lse, segment_ids, attn_in):
    length, width = q.shape
    half = full_spec((width // 2, 3 * LANES), 1)
    half_shape = shape_of((width // 2, 3 * LANES), bf16)
    sliced = pl.BlockSpec((length, LANES), lambda i: (0, which))
    out = full_spec((length, LANES), 1)
    act = shape_of((length, LANES), bf16)
    return pl.pallas_call(
        attend_back_kernel,
        grid=(1,),
        in_specs=[
            smem(), sliced, sliced, sliced, sliced,
            pl.BlockSpec((1, 8, length), lambda i: (which, 0, 0)), full_spec((1, length)),
            full_spec((length, width), 1),
        ],
        out_specs=[out, out, out, half, half],
        out_shape=[act, act, act, half_shape, half_shape],
        scratch_shapes=[
            pltpu.VMEM((WINDOW, length), f32),
            pltpu.VMEM((length, LANES), f32), pltpu.VMEM((length, LANES), f32),
            pltpu.VMEM((width, 3 * LANES), f32),
        ],
        cost_estimate=cost(10e9, 4e6, 2e6),
        name="attend_backward_%d" % which,
    )(here, q, k, v, do, lse, segment_ids, attn_in)


def project_kernel(x_ref, o_ref, wo_ref, gain_ref, bias_ref, y_ref, h_ref):
    resid = x_ref[...].astype(f32) + dot(o_ref[...], wo_ref[...])
    hat, _ = norm_parts(resid)
    y_ref[...] = resid
    h_ref[...] = (hat * gain_ref[...] + bias_ref[...]).astype(bf16)


def project(tokens, o, wo, gain, bias):
    length, width = tokens.shape
    rows = 256
    block = pl.BlockSpec((rows, width), lambda i: (i, 0))
    return pl.pallas_call(
        project_kernel,
        grid=(length // rows,),
        in_specs=[block, block, full_spec((width, width)), full_spec((1, width)), full_spec((1, width))],
        out_specs=[block, block],
        out_shape=[shape_of((length, width), f32), shape_of((length, width), bf16)],
        cost_estimate=cost(1.3e9, 9e6),
        name="project",
    )(tokens, o, wo, gain, bias)


def slots_kernel(capacity, groups, local, me_ref, counts_ref, order_ref, slot_ref):
    tokens = order_ref.shape[1]
    me = me_ref[0, 0]
    place = lax.broadcasted_iota(jnp.int32, (1, tokens), 1)
    slot = jnp.zeros((1, tokens), jnp.int32)
    lower = jnp.int32(0)
    for expert in range(groups * local):
        count = counts_ref[0, expert]
        base = ((expert % local) * groups + lax.bitwise_xor(me, expert // local)) * capacity - lower
        inside = (place >= lower) & (place < lower + count)
        slot = jnp.where(inside, place + base, slot)
        lower = lower + count
    order_col = column(order_ref[...])
    slot_col = column(slot)
    place_f = place.astype(f32)
    total = jnp.zeros((1, tokens), f32)
    step = 256
    for first in range(0, tokens, step):
        hit = order_col[first : first + step] == place_f
        total = total + jnp.sum(jnp.where(hit, slot_col[first : first + step], 0.0), axis=0, keepdims=True)
    slot_ref[...] = total.astype(jnp.int32)


def token_slots(me, counts, order, capacity, groups, local):
    tokens = order.shape[1]
    return pl.pallas_call(
        functools.partial(slots_kernel, capacity, groups, local),
        in_specs=[smem(), smem(), pl.BlockSpec(memory_space=pltpu.VMEM)],
        out_specs=pl.BlockSpec(memory_space=pltpu.VMEM),
        out_shape=shape_of((1, tokens), jnp.int32),
        cost_estimate=cost(4e6, 1e4),
        name="token_slots",
    )(me, counts, order)


def dispatch_kernel(capacity, groups, pieces, counted, slot_ref, counts_ref, *refs):
    sources = 1 + max(source for _, source in pieces)
    source_refs, out_refs = refs[:sources], refs[sources:]
    tokens, width = source_refs[0].shape
    rows = min(capacity * groups, 1024)
    for place, (own, source) in enumerate(pieces):
        at = slice(place * capacity, (place + 1) * capacity)
        for first in range(0, capacity * groups, rows):
            slot = lax.broadcasted_iota(jnp.int32, (rows, tokens), 0) + (own * groups * capacity + first)
            hit = jnp.where(slot == slot_ref[...], 1.0, 0.0).astype(bf16)
            found = dot(hit, source_refs[source][...]).astype(bf16)
            for part in range(rows // capacity):
                out_refs[first // capacity + part][at, :] = found[part * capacity : (part + 1) * capacity, :]
    if counted:
        experts = counts_ref.shape[1]
        counts = jnp.broadcast_to(counts_ref[...].astype(f32), (COUNT_ROWS, experts)).astype(bf16)
        for out_ref in out_refs:
            out_ref[len(pieces) * capacity :, :] = jnp.zeros((COUNT_ROWS, width), bf16)
            out_ref[len(pieces) * capacity :, :experts] = counts


def dispatch(pieces, counted, slots, counts, sources, capacity, groups):
    width = sources[0].shape[1]
    rows = len(pieces) * capacity + COUNT_ROWS * counted
    vmem = pl.BlockSpec(memory_space=pltpu.VMEM)
    return list(pl.pallas_call(
        functools.partial(dispatch_kernel, capacity, groups, pieces, counted),
        in_specs=[vmem] * (2 + len(sources)),
        out_specs=[vmem] * groups,
        out_shape=[shape_of((rows, width), bf16)] * groups,
        cost_estimate=cost(2e9, 3e6),
        name="dispatch_%d" % pieces[0][0],
    )(slots, counts, *sources))


def collect_kernel(capacity, groups, own, slot_ref, *refs):
    part_refs, out_ref, all_parts = refs[:groups], refs[groups], refs[groups + 1]
    for which in range(groups):
        all_parts[which * capacity : (which + 1) * capacity, :] = part_refs[which][...]
    out_ref[...] = collected(slot_ref[...], all_parts[...], own).astype(bf16)


def collected(slot_row, parts, own):
    slot_col = column(slot_row).astype(jnp.int32)
    shape = (slot_col.shape[0], parts.shape[0])
    slot = lax.broadcasted_iota(jnp.int32, shape, 1) + own * parts.shape[0]
    return dot(jnp.where(slot == slot_col, 1.0, 0.0).astype(bf16), parts)


def collect(own, slots, parts, capacity, half=0):
    groups, width = len(parts), parts[0].shape[1]
    tokens = slots.shape[1]
    return pl.pallas_call(
        functools.partial(collect_kernel, capacity, groups, own),
        grid=(1,),
        in_specs=[full_spec((1, tokens), 1)]
        + [pl.BlockSpec((capacity, width), lambda i: (half, 0), pipeline_mode=pl.Buffered(1))] * groups,
        out_specs=full_spec((tokens, width), 1),
        out_shape=shape_of((tokens, width), bf16),
        scratch_shapes=[pltpu.VMEM((groups * capacity, width), bf16)],
        cost_estimate=cost(2e9, 3e6),
        name="collect_%d" % own,
    )(slots, *parts)


def gelu_parts(pre):
    cdf = 0.5 * (1.0 + lax.erf(pre * ROOT_HALF))
    density = NORMAL_PEAK * jnp.exp(-0.5 * pre * pre)
    return pre * cdf, cdf + pre * density


def expert_kernel(capacity, groups, local, own, joined, rows2, me_ref, counts_ref, router_ref, *refs):
    h_refs, g_refs = refs[:groups], refs[groups : 2 * groups]
    w1_ref, w2_ref = refs[2 * groups : 2 * groups + 2]
    refs = refs[2 * groups + 2 :]
    if joined:
        dh_refs = [ref.at[:capacity] for ref in refs[:groups]]
        z_refs = [ref.at[capacity:] for ref in refs[:groups]]
        refs = refs[groups:]
    else:
        dh_refs, z_refs = refs[:groups], refs[groups : 2 * groups]
        refs = refs[2 * groups :]
    dw_ref = refs[0]
    h_all, g_all, gz_all, h_turned, gate_all, z_sum, du_sum, z_low, dh_low, w1_stage, w2_stage, sems = refs[1:]
    slab = capacity * groups
    piece = 256
    step = pl.program_id(0)
    expert = me_ref[0, 0] * local + own
    starts = []
    lower = jnp.int32(0)
    for source in range(groups):
        starts.append(pl.multiple_of(lower, 16))
        lower = lower + (counts_ref[source, expert] + 15) // 16 * 16
    pieces = jnp.maximum((lower + piece - 1) // piece, 1)
    router = router_ref[pl.ds(expert, 1), :]

    _, shards_count, rows1, block = w1_stage.shape
    width = w2_stage.shape[2]
    sub = math.gcd(block, rows2)
    per_slab = width // block

    def copies(at, slot):
        found = [
            pltpu.make_async_copy(
                w1_stage.at[slot],
                dw_ref.at[
                    :,
                    pl.ds(pl.multiple_of(rows2 + at // per_slab * rows1, 16), rows1),
                    pl.ds(pl.multiple_of(at % per_slab * block, 128), block),
                ],
                sems.at[slot, 0],
            )
        ]
        for which in range(block // sub):
            place = at * (block // sub) + which
            shard = place * sub // rows2
            row = pl.multiple_of(place * sub - shard * rows2, 16)
            found.append(
                pltpu.make_async_copy(
                    w2_stage.at[slot, pl.ds(which * sub, sub)],
                    dw_ref.at[shard, pl.ds(row, sub)],
                    sems.at[slot, 1 + which],
                )
            )
        return found

    @pl.when(step == 0)
    def _():
        h_all[...] = jnp.zeros_like(h_all)
        g_all[...] = jnp.zeros_like(g_all)
        z_sum[...] = jnp.zeros_like(z_sum)
        du_sum[...] = jnp.zeros_like(du_sum)
        for source in range(groups):
            h_all[pl.ds(starts[source], capacity), :] = h_refs[source][...]
            g_all[pl.ds(starts[source], capacity), :] = g_refs[source][...]
        for first in range(0, slab, piece):
            rows = slice(first, first + piece)
            h = h_all[rows, :]
            gate = jax.nn.sigmoid(jnp.sum(h.astype(f32) * router, axis=1, keepdims=True))
            gate_all[rows, :] = jnp.broadcast_to(gate, (piece, 128))
            gz_all[rows, :] = (gate * g_all[rows, :].astype(f32)).astype(bf16)
            h_turned[:, rows] = h.T

    slot = lax.rem(step, 2)

    @pl.when(step >= 2)
    def _():
        for copy in copies(step - 2, slot):
            copy.wait()

    for count in range(1, slab // piece + 1):

        @pl.when(pieces == count)
        def _():
            rows = slice(0, count * piece)
            h, gz = h_all[rows, :], gz_all[rows, :]
            w1, w2 = w1_ref[0], w2_ref[0]
            hid, slope = gelu_parts(dot(h, w1))
            hid = hid.astype(bf16)
            z_sum[rows, :] += dot(hid, w2)
            dpre = (dot_nt(gz, w2) * slope).astype(bf16)
            w2_stage[slot] = dot_tn(hid, gz).astype(bf16)
            w1_stage[slot] = dot(h_turned[:, rows], dpre).astype(bf16).reshape(shards_count, rows1, block)
            du_sum[rows, :] += dot_nt(dpre, w1)

    for copy in copies(step, slot):
        copy.start()

    @pl.when(step == pl.num_programs(0) - 1)
    def _():
        for first in range(0, slab, piece):
            rows = slice(first, first + piece)
            gate = gate_all[rows, :1]
            z = z_sum[rows, :]
            dlogit = jnp.sum(g_all[rows, :].astype(f32) * z, axis=1, keepdims=True) * gate * (1.0 - gate)
            z_low[rows, :] = (gate * z).astype(bf16)
            dh_low[rows, :] = (du_sum[rows, :] + dlogit * router).astype(bf16)
        for source in range(groups):
            z_refs[source][...] = z_low[pl.ds(starts[source], capacity), :]
            dh_refs[source][...] = dh_low[pl.ds(starts[source], capacity), :]
        for copy in copies(step - 1, 1 - slot) + copies(step, slot):
            copy.wait()


def run_expert(own, me, counts, router, h_parts, g_parts, expert_in, expert_out, capacity, joined):
    groups = len(h_parts)
    local, width, hidden = expert_in.shape
    shards_count = lax.axis_size("dp")
    slab = capacity * groups
    block = 256
    rows1, rows2 = width // shards_count, hidden // shards_count
    h_part = pl.BlockSpec((capacity, width), lambda f: (0, 0), pipeline_mode=pl.Buffered(1))
    g_part = pl.BlockSpec((capacity, width), lambda f: (own, 0), pipeline_mode=pl.Buffered(1))
    ends = groups if joined else 2 * groups
    end_rows = 2 * capacity if joined else capacity
    results = pl.pallas_call(
        functools.partial(expert_kernel, capacity, groups, local, own, joined, rows2),
        grid=(hidden // block,),
        in_specs=[smem(), smem(), full_spec(router.shape)] + [h_part] * groups + [g_part] * groups + [
            pl.BlockSpec((1, width, block), lambda f: (own, 0, f)),
            pl.BlockSpec((1, block, width), lambda f: (own, f, 0)),
        ],
        out_specs=[full_spec((end_rows, width), 1)] * ends + [pl.BlockSpec(memory_space=pl.ANY)],
        out_shape=[shape_of((end_rows, width), bf16)] * ends
        + [shape_of((shards_count, rows2 + rows1 * (hidden // width), width), bf16)],
        scratch_shapes=[
            pltpu.VMEM((slab, width), bf16), pltpu.VMEM((slab, width), bf16),
            pltpu.VMEM((slab, width), bf16), pltpu.VMEM((width, slab), bf16),
            pltpu.VMEM((slab, 128), f32),
            pltpu.VMEM((slab, width), f32), pltpu.VMEM((slab, width), f32),
            pltpu.VMEM((slab, width), bf16), pltpu.VMEM((slab, width), bf16),
            pltpu.VMEM((2, shards_count, rows1, block), bf16), pltpu.VMEM((2, block, width), bf16),
            pltpu.SemaphoreType.DMA((2, 1 + block // math.gcd(block, rows2))),
        ],
        cost_estimate=cost(25e9, 25e6, 6e6),
        name="expert_%d" % own,
    )(me, counts, router, *h_parts, *g_parts, expert_in, expert_out)
    return results[:-1], results[-1]


def shares_kernel(rows1, rows2, has_before, share_ref, *refs):
    first_ref, second_ref = refs[2:] if has_before else refs
    width = share_ref.shape[1]
    second_ref[0] = share_ref[:rows2, :].astype(f32)
    for slab in range(first_ref.shape[2] // width):
        rows = slice(rows2 + slab * rows1, rows2 + (slab + 1) * rows1)
        first_ref[0, :, slab * width : (slab + 1) * width] = share_ref[rows, :].astype(f32)


def unpack_shares(own, share, before, local, rows1, rows2, hidden):
    width = share.shape[1]
    anywhere = pl.BlockSpec(memory_space=pl.ANY)
    return pl.pallas_call(
        functools.partial(shares_kernel, rows1, rows2, before is not None),
        grid=(1,),
        in_specs=[full_spec(share.shape, 1)] + ([] if before is None else [anywhere, anywhere]),
        out_specs=[
            pl.BlockSpec((1, rows1, hidden), lambda i: (own, 0, 0)),
            pl.BlockSpec((1, rows2, width), lambda i: (own, 0, 0)),
        ],
        out_shape=[shape_of((local, rows1, hidden), f32), shape_of((local, rows2, width), f32)],
        input_output_aliases={} if before is None else {1: 0, 2: 1},
        cost_estimate=cost(1, 1),
        name="unpack_shares",
    )(share, *([] if before is None else before))


def norm2_kernel(
    here_ref, dh0_ref, dh1_ref, y_ref, g_ref, o_ref, wo_ref, gain_ref,
    dy_ref, do_ref, keep_ref, send_ref, vec_ref, dwo_sum, gain_sum, bias_sum,
):
    step = pl.program_id(0)

    @pl.when(step == 0)
    def _():
        dwo_sum[...] = jnp.zeros_like(dwo_sum)
        gain_sum[...] = jnp.zeros_like(gain_sum)
        bias_sum[...] = jnp.zeros_like(bias_sum)

    dh = dh0_ref[...].astype(f32) + dh1_ref[...].astype(f32)
    hat, inverse_std = norm_parts(y_ref[...])
    gain_sum[...] += jnp.sum(dh * hat, axis=0, keepdims=True)
    bias_sum[...] += jnp.sum(dh, axis=0, keepdims=True)
    dy = g_ref[...].astype(f32) + norm_back(dh, hat, inverse_std, gain_ref[...])
    dy_ref[...] = dy
    dyb = dy.astype(bf16)
    do_ref[...] = dot_nt(dyb, wo_ref[...]).astype(bf16)
    dwo_sum[...] += dot_tn(o_ref[...], dyb)

    @pl.when(step == pl.num_programs(0) - 1)
    def _():
        split_cores(here_ref[0, 1], dwo_sum, keep_ref, send_ref)
        vec_ref[0:1, :] = gain_sum[...]
        vec_ref[1:2, :] = bias_sum[...]


def norm2_back(here, dh_own, y, cotangent, o, wo, gain):
    length, width = y.shape
    rows = 256
    block = pl.BlockSpec((rows, width), lambda i: (i, 0))
    return pl.pallas_call(
        norm2_kernel,
        grid=(length // rows,),
        in_specs=[smem()] + [block] * 5 + [full_spec((width, width)), full_spec((1, width))],
        out_specs=[block, block] + [full_spec((width // 2, width), 1)] * 2 + [full_spec((2, width))],
        out_shape=[
            shape_of((length, width), f32), shape_of((length, width), bf16),
            shape_of((width // 2, width), bf16), shape_of((width // 2, width), bf16), shape_of((2, width), f32),
        ],
        scratch_shapes=[pltpu.VMEM((width, width), f32), pltpu.VMEM((1, width), f32), pltpu.VMEM((1, width), f32)],
        cost_estimate=cost(3e9, 15e6),
        name="norm2_back",
    )(here, *dh_own, y, cotangent, o, wo, gain)


def result_kernel(y_ref, z0_ref, z1_ref, out_ref):
    out_ref[...] = (y_ref[...] + (z0_ref[...].astype(f32) + z1_ref[...].astype(f32))).astype(bf16)


def block_result(y, z_own):
    length, width = y.shape
    rows = 256
    block = pl.BlockSpec((rows, width), lambda i: (i, 0))
    return pl.pallas_call(
        result_kernel,
        grid=(length // rows,),
        in_specs=[block] * 3,
        out_specs=block,
        out_shape=shape_of((length, width), bf16),
        cost_estimate=cost(3e6, 8e6),
        name="block_result",
    )(y, *z_own)


def norm1_kernel(cuts, here_ref, x_ref, dy_ref, wq_ref, wk_ref, wv_ref, gain_ref, vec2_ref, *refs):
    grad_refs = refs[: 3 * cuts]
    dx_ref, keep_ref, send_ref, vec_sum, gain_sum, bias_sum = refs[3 * cuts :]
    step = pl.program_id(0)

    @pl.when(step == 0)
    def _():
        gain_sum[...] = jnp.zeros_like(gain_sum)
        bias_sum[...] = jnp.zeros_like(bias_sum)

    da = None
    for which, w_ref in enumerate((wq_ref, wk_ref, wv_ref)):
        grad = jnp.concatenate([grad_refs[3 * cut + which][...] for cut in range(cuts)], axis=1)
        term = dot_nt(grad, w_ref[...])
        da = term if da is None else da + term
    hat, inverse_std = norm_parts(x_ref[...].astype(f32))
    gain_sum[...] += jnp.sum(da * hat, axis=0, keepdims=True)
    bias_sum[...] += jnp.sum(da, axis=0, keepdims=True)
    dx_ref[...] = (dy_ref[...] + norm_back(da, hat, inverse_std, gain_ref[...])).astype(bf16)

    @pl.when(step == pl.num_programs(0) - 1)
    def _():
        vec_sum[...] = jnp.zeros_like(vec_sum)
        vectors = jnp.concatenate(
            [gain_sum[...], bias_sum[...], vec2_ref[...], jnp.zeros((12, vec_sum.shape[1]), f32)], axis=0
        )
        high = vectors.astype(bf16).astype(f32)
        vec_sum[0:16, :] = high
        vec_sum[16:32, :] = vectors - high
        split_cores(here_ref[0, 1], vec_sum, keep_ref, send_ref)


def norm1_back(here, grads, tokens, dy, wq, wk, wv, gain, vec2):
    length, width = tokens.shape
    rows = 256
    cuts = len(grads)
    block = pl.BlockSpec((rows, width), lambda i: (i, 0))
    part = pl.BlockSpec((rows, width // cuts), lambda i: (i, 0))
    weight = full_spec((width, width))
    half = full_spec((VECTOR_ROWS, width), 1)
    half_shape = shape_of((VECTOR_ROWS, width), bf16)
    return pl.pallas_call(
        functools.partial(norm1_kernel, cuts),
        grid=(length // rows,),
        in_specs=[smem()] + [block] * 2 + [weight] * 3 + [full_spec((1, width)), full_spec((2, width))]
        + [part] * (3 * cuts),
        out_specs=[block, half, half],
        out_shape=[shape_of((length, width), bf16), half_shape, half_shape],
        scratch_shapes=[
            pltpu.VMEM((2 * VECTOR_ROWS, width), f32), pltpu.VMEM((1, width), f32), pltpu.VMEM((1, width), f32),
        ],
        cost_estimate=cost(8e9, 20e6),
        name="norm1_back",
    )(here, tokens, dy, wq, wk, wv, gain, vec2, *[grad for three in grads for grad in three])


def swap(array, axis, step):
    count = lax.axis_size(axis)
    return lax.ppermute(array, axis, [(i, i ^ step) for i in range(count)])


def add_picked_kernel(sets, terms, outs, me_ref, *refs):
    me = me_ref[0, 0]
    for step in range(outs):
        index = lax.bitwise_xor(me, step)
        out_ref = refs[sets * terms + step]
        row = 0
        for which in range(sets):
            total = refs[which * terms][index].astype(f32)
            for ref in refs[which * terms + 1 : (which + 1) * terms]:
                total = total + ref[index].astype(f32)
            out_ref[row : row + total.shape[0], :] = total.astype(bf16)
            row += total.shape[0]


def add_picked(sets, pieces, me, name):
    width = sets[0][0].shape[1]
    arrays = [array.reshape(pieces, array.shape[0] // pieces, width) for terms in sets for array in terms]
    rows = sum(terms[0].shape[0] // pieces for terms in sets)
    vmem = pl.BlockSpec(memory_space=pltpu.VMEM)
    return list(pl.pallas_call(
        functools.partial(add_picked_kernel, len(sets), len(sets[0]), pieces),
        in_specs=[smem()] + [vmem] * len(arrays),
        out_specs=[vmem] * pieces,
        out_shape=[shape_of((rows, width), bf16)] * pieces,
        cost_estimate=cost(1, 1),
        name=name,
    )(me, *arrays))


def fold_order(count):
    if count == 1:
        return [0]
    inner = fold_order(count // 2)
    return [2 * place for place in inner] + [2 * place + 1 for place in inner]


def add_halves_kernel(me_ref, *refs):
    terms, out_refs = refs[:-2], refs[-2:]
    count, rows, _ = terms[0].shape
    for at, step in enumerate(fold_order(count)):
        index = lax.bitwise_xor(me_ref[0, 0], step)
        total = terms[0][index].astype(f32)
        for ref in terms[1:]:
            total = total + ref[index].astype(f32)
        first = at % (count // 2) * rows
        out_refs[at // (count // 2)][first : first + rows, :] = total.astype(bf16)


def add_halves(terms, pieces, me):
    width = terms[0].shape[1]
    rows = terms[0].shape[0] // pieces
    vmem = pl.BlockSpec(memory_space=pltpu.VMEM)
    return list(pl.pallas_call(
        add_halves_kernel,
        in_specs=[smem()] + [vmem] * len(terms),
        out_specs=[vmem] * 2,
        out_shape=[shape_of((pieces * rows // 2, width), bf16)] * 2,
        cost_estimate=cost(1, 1),
        name="add_halves",
    )(me, *[term.reshape(pieces, rows, width) for term in terms]))


def add_kernel(first_ref, second_ref, *out_refs):
    total = (first_ref[...].astype(f32) + second_ref[...].astype(f32)).astype(bf16)
    rows = out_refs[0].shape[0]
    for at, out_ref in enumerate(out_refs):
        out_ref[...] = total[at * rows : (at + 1) * rows, :]


def add_two(first, second, outs):
    rows, width = first.shape
    vmem = pl.BlockSpec(memory_space=pltpu.VMEM)
    return list(pl.pallas_call(
        add_kernel,
        in_specs=[vmem] * 2,
        out_specs=[vmem] * outs,
        out_shape=[shape_of((rows // outs, width), bf16)] * outs,
        cost_estimate=cost(1, 1),
        name="add_two",
    )(first, second))


def line_kernel(sizes, me_ref, *refs):
    count = len(refs) - 1
    for step in range(count):
        place = lax.bitwise_xor(me_ref[0, 0], step)
        row, start = 0, 0
        for size in sizes:
            at = pl.multiple_of(start + place * size, 8)
            refs[count][pl.ds(at, size), :] = refs[step][row : row + size, :]
            row += size
            start += size * count


def line_up(arrays, sizes, me):
    vmem = pl.BlockSpec(memory_space=pltpu.VMEM)
    count = len(arrays)
    rows, width = arrays[0].shape
    if any(size % 8 for size in sizes):
        ordered = jnp.stack(arrays)[lax.bitwise_xor(me[0, 0], jnp.arange(count, dtype=jnp.int32))]
        starts = [sum(sizes[:which]) for which in range(len(sizes))]
        return jnp.concatenate(
            [ordered[:, start : start + size].reshape(-1, width) for start, size in zip(starts, sizes)]
        )
    return pl.pallas_call(
        functools.partial(line_kernel, sizes),
        in_specs=[smem()] + [vmem] * count,
        out_specs=vmem,
        out_shape=shape_of((count * rows, width), bf16),
        cost_estimate=cost(1, 1),
        name="line_up",
    )(me, *arrays)


def finish_kernel(groups, here_ref, *refs):
    count = 2 * groups
    first_lines, last_lines, refs = refs[:count], refs[count : 2 * count], refs[2 * count :]
    out_ref, head_refs, vec_ref, vec_all = refs[0], refs[1:4], refs[4], refs[5]
    me, core = here_ref[0, 0], here_ref[0, 1]
    width = out_ref.shape[0]
    size = width // (2 * groups)
    vec_size = VECTOR_ROWS // groups
    for side in range(2):
        for step in range(groups):
            first, last = first_lines[side * groups + step], last_lines[side * groups + step]
            index = lax.bitwise_xor(core, side) * groups + lax.bitwise_xor(me, step)
            rows = pl.ds(pl.multiple_of(index * size, 8), size)
            out_ref[rows, :] = first[:size, :].astype(f32)
            cuts = width // LANES
            for cut in range(cuts):
                block = last[:size, :] if cut == cuts - 1 else first[(cut + 1) * size : (cut + 2) * size, :]
                block = block.astype(f32)
                for which in range(3):
                    head_refs[which][rows, cut * LANES : (cut + 1) * LANES] = (
                        block[:, which * LANES : (which + 1) * LANES]
                    )
            vec_all[pl.ds(pl.multiple_of(index * vec_size, 8), vec_size), :] = (
                last[size : size + vec_size, :].astype(f32)
            )
    vec_ref[...] = vec_all[0:8, :] + vec_all[16:24, :]


def finish(first_lines, last_lines, width, groups, here):
    vmem = pl.BlockSpec(memory_space=pltpu.VMEM)
    return pl.pallas_call(
        functools.partial(finish_kernel, groups),
        in_specs=[smem()] + [vmem] * (4 * groups),
        out_specs=[vmem] * 5,
        out_shape=[shape_of((width, width), f32)] * 4 + [shape_of((8, width), f32)],
        scratch_shapes=[pltpu.VMEM((2 * VECTOR_ROWS, width), f32)],
        cost_estimate=cost(1, 1),
        name="finish",
    )(here, *first_lines, *last_lines)


def shards(
    tokens, segment_ids, expert_order, expert_counts, norm1_gain, norm1_bias,
    query_w, key_w, value_w, out_w, norm2_gain, norm2_bias, router_w,
    expert_in, expert_out, cotangent,
):
    groups = lax.axis_size("expert")
    local = expert_in.shape[0]
    experts = expert_counts.shape[1]
    length, width = tokens.shape
    capacity = 2 * length // experts
    me_index = lax.axis_index("expert").astype(jnp.int32)
    me = me_index.reshape(1, 1)
    depth = lax.axis_size("dp") // 2
    core_index = (lax.axis_index("dp") % 2).astype(jnp.int32)
    here = jnp.stack([me_index, core_index]).reshape(1, 2)
    place = (lax.axis_index("dp") // 2).astype(jnp.int32).reshape(1, 1)
    gain1, bias1 = norm1_gain.reshape(1, width), norm1_bias.reshape(1, width)
    gain2, bias2 = norm2_gain.reshape(1, width), norm2_bias.reshape(1, width)
    router = router_w.T.astype(f32)

    def exchange(parts):
        return [parts[0]] + [swap(parts[step], "expert", step) for step in range(1, groups)]

    barrier = lax.optimization_barrier
    slots = token_slots(me, expert_counts, expert_order.reshape(1, length), capacity, groups, local)
    pieces = tuple((own, 0) for own in range(local))
    g_parts = exchange(dispatch(pieces, True, slots, expert_counts, [cotangent], capacity, groups))
    attn_in, q, k, v, o, lse = attend_forward(tokens, gain1, bias1, query_w, key_w, value_w, segment_ids)
    y, h = project(tokens, o, out_w, gain2, bias2)
    h, g_parts = barrier((h, g_parts))
    row = local * capacity
    counts_all = jnp.concatenate([part[row : row + 1, :experts] for part in g_parts]).astype(jnp.int32)
    outgoing = [dispatch(((own, 0),), False, slots, expert_counts, [h], capacity, groups) for own in range(local)]
    incoming = [exchange(out) for out in outgoing]
    incoming[0], _ = barrier((incoming[0], outgoing))

    def expert(own, joined):
        return run_expert(
            own, me, counts_all, router, incoming[own], g_parts, expert_in, expert_out, capacity, joined
        )

    def scatter(array):
        share = lax.psum_scatter(array, "dp", scatter_dimension=0, tiled=True)
        return share.reshape(share.shape[1:])

    joined_ins, grads_out = [], []
    for own in range(local - 1):
        out, dw = expert(own, True)
        dw, incoming[own + 1] = barrier((dw, incoming[own + 1]))
        incoming[own + 1], _ = barrier((incoming[own + 1], out))
        grads_out.append(scatter(dw))
        joined_ins.append(exchange(out))
    own = local - 1
    out, dw_last = expert(own, False)
    dh_out, z_out = out[:groups], out[groups:]
    dh_in = exchange(dh_out)
    dh_own, z_own = [], []
    for before in range(own):
        joined_ins[before], _ = barrier((joined_ins[before], dh_out))
        dh_own.append(collect(before, slots, joined_ins[before], capacity))
        z_own.append(collect(before, slots, joined_ins[before], capacity, 1))
    dh_in, _ = barrier((dh_in, dh_own + z_own))
    dh_own.append(collect(own, slots, dh_in, capacity))
    dh_own, dw_last, z_out = barrier((dh_own, dw_last, z_out))
    grads_out.append(scatter(dw_last))
    z_in = exchange(z_out)
    def spread(parts, axis, stride=1):
        return [parts[0]] + [swap(parts[step], axis, stride * step) for step in range(1, len(parts))]

    dy, do, keep_out, send_out, vec2 = norm2_back(here, dh_own, y, cotangent, o, out_w, gain2)
    kept, came = [keep_out], [swap(send_out, "dp", 1)]
    grads = []
    for which in range(width // LANES):
        *grad, keep, send = attend_backward(which, here, q, k, v, do, lse, segment_ids, attn_in)
        send, grad, q = barrier((send, grad, q))
        grads.append(grad)
        kept.append(keep)
        came.append(swap(send, "dp", 1))
    def after(value, *earlier):
        return barrier((value, earlier))[0]

    def unpack(which, share, shares):
        return unpack_shares(
            which, share, shares, local, width // lax.axis_size("dp"),
            expert_in.shape[2] // lax.axis_size("dp"), expert_in.shape[2],
        )

    first = [[keep, other] for keep, other in zip(kept[:-1], after(came[:-1], send, z_in))]
    first = add_picked(first, groups, here, "add_cores")
    first_came = spread(first, "expert")
    dx, keep, send = norm1_back(
        here, after(grads, first[0]), tokens, dy, query_w, key_w, value_w, gain1, vec2
    )
    other = swap(send, "dp", 1)
    z_own.append(collect(own, after(slots, send), z_in, capacity))
    bits = [1 << bit for bit in range(depth.bit_length() - 1)]

    def lined(mine):
        held = [mine]
        for bit in reversed(bits):
            held = held + [swap(part, "dp", 2 * bit) for part in held]
        ordered = [None] * depth
        for at, part in enumerate(held):
            place = sum(bit for which, bit in enumerate(reversed(bits)) if at >> which & 1)
            ordered[place] = part
        return ordered

    keep_first, send_first = add_halves(after(first_came, z_own[-1]), depth, place)
    other_first = swap(send_first, "dp", 2)
    last = [[kept[-1], after(came[-1], send_first)], [keep, other]]
    last = add_picked(last, groups, here, "add_cores")
    last_came = spread(last, "expert")
    for bit in bits[1:]:
        keep_first, send_first = add_two(keep_first, after(other_first, last[0]), 2)
        other_first = swap(send_first, "dp", 2 * bit)
    block_out = block_result(after(y, (last[0], send_first)), z_own)
    first = add_two(keep_first, after(other_first, block_out), 1)[0]
    first_came = lined(first)
    keep_last, send_last = add_halves(after(last_came, first), depth, place)
    other_last = swap(send_last, "dp", 2)
    first = line_up(after(first_came, send_last), [first.shape[0]], place)
    first_plane = spread([first] * groups, "expert")
    for bit in bits[1:]:
        keep_last, send_last = add_two(keep_last, after(other_last, first), 2)
        other_last = swap(send_last, "dp", 2 * bit)
    shares = None
    for which in range(local - 1):
        shares = unpack(which, after(grads_out[which], send_last), shares)
    last = add_two(keep_last, after(other_last, shares), 1)[0]
    last_came = lined(last)
    last = line_up(last_came, [last.shape[0]], place)
    last_plane = spread([last] * groups, "expert")
    first_lines = first_plane + [swap(part, "dp", 1) for part in after(first_plane, last)]
    last_lines = last_plane + [swap(part, "dp", 1) for part in last_plane]
    grad_o, grad_q, grad_k, grad_v, vectors = finish(first_lines, last_lines, width, groups, here)
    shares = unpack(local - 1, grads_out[local - 1], shares)
    return (
        block_out,
        dx,
        vectors[0],
        vectors[1],
        grad_q,
        grad_k,
        grad_v,
        grad_o,
        vectors[2],
        vectors[3],
        shares[0],
        shares[1],
    )


def solution(mesh):
    placed = (
        P(("dp", "expert"), None), P(("dp", "expert"), None), P(("dp", "expert")), P(("dp", "expert"), None),
        P(), P(), P(), P(), P(), P(), P(), P(), P(),
        P("expert", None, None), P("expert", None, None), P(("dp", "expert"), None),
    )
    return jax.shard_map(
        shards,
        mesh=mesh,
        in_specs=placed,
        out_specs=(
            P(("dp", "expert"), None), P(("dp", "expert"), None),
            P(), P(), P(), P(), P(), P(), P(), P(),
            P("expert", "dp", None), P("expert", "dp", None),
        ),
        check_vma=False,
    )
```
